32 devices in a mesh: branch: 2 (over y), res: 16 (over z, x, core).
Axes of the slice: x: 2, y: 2, z: 4, core: 2. Of those that a mesh axis runs over, the one named last changes fastest.
Arguments:
- alignment_representation: float32 [128, 96, 256], P(None, 'res'), may hold values from -6 to 6
- pairwise_state: float32 [96, 96, 128], P('res'), may hold values from -6 to 6
- alignment_mask: int32 [128, 96], P(None, 'res'), may hold values from 0 to 1, as said below
- residue_present_mask: int32 [96], P('res'), may hold values from 0 to 1, as said below
- row_projection_weight: float32 [4, 256, 256], replicated
- lateral_result_coeffs: float32 [256, 256], replicated, may hold values from -1.5 to 1.5
- pair_bias_weight: float32 [128, 8], replicated, may hold values from -0.75 to 0.75
- first_operand_coeffs: float32 [256, 32], replicated, may hold values from -0.375 to 0.375
- other_operand_coeffs: float32 [256, 32], replicated, may hold values from -0.375 to 0.375
- outer_output_weight: float32 [1024, 128], replicated, may hold values from -2 to 2
- starting_projection_weight: float32 [4, 128, 128], replicated
- starting_bias_weight: float32 [128, 4], replicated, may hold values from -0.75 to 0.75
- starting_output_weight: float32 [128, 128], replicated, may hold values from -2 to 2
- ending_projection_weight: float32 [4, 128, 128], replicated
- ending_bias_weight: float32 [128, 4], replicated, may hold values from -0.75 to 0.75
- ending_output_weight: float32 [128, 128], replicated, may hold values from -2 to 2
Outputs:
- alignment_output: float32 [128, 96, 256], P('branch', 'res')
- pairwise_output: float32 [96, 96, 128], P('res', None, 'branch')
The draws below stay inside these ranges and needn't reach their ends.
Inputs may be any that keep to these rules, and one draw needn't show every extreme that they name: residue_present_mask is 1 on the first L residues and 0 on the rest, for a drawn L from 48 to 96. alignment_mask[s, r] is 1 exactly where s is below a drawn count from 32 to 128 and residue_present_mask[r] is 1.
All inputs are finite; a program needn't handle non-finite values.
Results may differ from the reference program's by a relative error of at most 0.0003.
Values sent between devices are 32-bit elements; how exact they have to be, the bound alone decides.
A program may use at most 128 MiB of HBM per device.

```python
import math
import jax
import jax.numpy as jnp
from jax import lax

ALIGNED_FEATURES = 256
C_Z = 128
ATTEND_HEADS = 8
HEADS_Z = 4
PRODUCT_WIDTH = 32
ALIGNED_CHAINS = 128
CUT_AMINO_COUNT = 96


def mask_counts(key):
    starting_amount = jax.random.fold_in(key, 7)
    live_res = jax.random.randint(jax.random.fold_in(starting_amount, 1), (), CUT_AMINO_COUNT // 2, CUT_AMINO_COUNT + 1)
    valid_chain_indicator = jax.random.randint(jax.random.fold_in(starting_amount, 2), (), ALIGNED_CHAINS // 4, ALIGNED_CHAINS + 1)
    return (live_res, valid_chain_indicator)


def draw_residue_present_mask(key, part):
    live_res, valid_chain_indicator = mask_counts(key)
    return (jnp.arange(CUT_AMINO_COUNT) < live_res).astype(jnp.int32)


def draw_alignment_mask(key, part):
    live_res, valid_chain_indicator = mask_counts(key)
    chain_share_slice = jnp.arange(ALIGNED_CHAINS)[:, None] < valid_chain_indicator
    res_part = jnp.arange(CUT_AMINO_COUNT)[None, :] < live_res
    return (chain_share_slice & res_part).astype(jnp.int32)


def rescaled_mapping(key, salt, channels):
    own_key = jax.random.fold_in(key, salt)
    starting_amount = jax.random.normal(jax.random.fold_in(own_key, 1), (4, channels, channels), jnp.float32) / math.sqrt(channels)
    return starting_amount


def draw_row_projection_weight(key, part):
    return rescaled_mapping(key, 101, ALIGNED_FEATURES)


def draw_starting_projection_weight(key, part):
    return rescaled_mapping(key, 202, C_Z)


def draw_ending_projection_weight(key, part):
    return rescaled_mapping(key, 303, C_Z)


def block_levels(rng, shape, shards, low, top_value):
    def one(axis_at, shards_of):
        draws = jax.random.uniform(jax.random.fold_in(jax.random.fold_in(rng, 6), axis_at), (shards_of,), jnp.float32, low / len(shards), top_value / len(shards))
        return jnp.repeat(jnp.exp(draws), shape[axis_at] // shards_of).reshape((-1,) + (1,) * (len(shape) - axis_at - 1))

    level = one(*shards[0])
    for cut in shards[1:]:
        level = level * one(*cut)
    return level


def normal_values(key, shape, width, limit, split=(), kind=jnp.bfloat16):
    level = block_levels(key, shape, split, -0.22, 0.18) if split else 1.0
    result = jax.random.normal(key, shape, jnp.float32) * width * level
    return jnp.minimum(jnp.maximum(result, -limit), limit).astype(kind)


def setup_inputs(seed: int = 0) -> dict:
    key_of = jax.random.split(jax.random.key(seed), 17)
    alignment_representation = normal_values(key_of[0], (ALIGNED_CHAINS, CUT_AMINO_COUNT, ALIGNED_FEATURES), 1.0, 6.0, ((1, 16),), jnp.float32)
    pairwise_state = normal_values(key_of[1], (CUT_AMINO_COUNT, CUT_AMINO_COUNT, C_Z), 1.0, 6.0, ((0, 16),), jnp.float32)
    alignment_mask = draw_alignment_mask(jax.random.fold_in(key_of[16], 71), 0)
    residue_present_mask = draw_residue_present_mask(jax.random.fold_in(key_of[16], 71), 0)
    row_projection_weight = draw_row_projection_weight(jax.random.fold_in(key_of[16], 71), 0)
    lateral_result_coeffs = normal_values(key_of[5], (ALIGNED_FEATURES, ALIGNED_FEATURES), (ALIGNED_FEATURES // 16) ** -0.5, 1.5, (), jnp.float32)
    pair_bias_weight = normal_values(key_of[6], (C_Z, ATTEND_HEADS), (C_Z // 2) ** -0.5, 0.75, (), jnp.float32)
    first_operand_coeffs = normal_values(key_of[7], (ALIGNED_FEATURES, PRODUCT_WIDTH), ALIGNED_FEATURES ** -0.5, 0.375, (), jnp.float32)
    other_operand_coeffs = normal_values(key_of[8], (ALIGNED_FEATURES, PRODUCT_WIDTH), ALIGNED_FEATURES ** -0.5, 0.375, (), jnp.float32)
    outer_output_weight = normal_values(key_of[9], (PRODUCT_WIDTH * PRODUCT_WIDTH, C_Z), (PRODUCT_WIDTH // 4) ** -0.5, 2.0, (), jnp.float32)
    starting_projection_weight = draw_starting_projection_weight(jax.random.fold_in(key_of[16], 71), 0)
    starting_bias_weight = normal_values(key_of[11], (C_Z, HEADS_Z), (C_Z // 2) ** -0.5, 0.75, (), jnp.float32)
    starting_output_weight = normal_values(key_of[12], (C_Z, C_Z), (C_Z // 16) ** -0.5, 2.0, (), jnp.float32)
    ending_projection_weight = draw_ending_projection_weight(jax.random.fold_in(key_of[16], 71), 0)
    ending_bias_weight = normal_values(key_of[14], (C_Z, HEADS_Z), (C_Z // 2) ** -0.5, 0.75, (), jnp.float32)
    ending_output_weight = normal_values(key_of[15], (C_Z, C_Z), (C_Z // 16) ** -0.5, 2.0, (), jnp.float32)
    return {"alignment_representation": alignment_representation, "pairwise_state": pairwise_state, "alignment_mask": alignment_mask, "residue_present_mask": residue_present_mask, "row_projection_weight": row_projection_weight, "lateral_result_coeffs": lateral_result_coeffs, "pair_bias_weight": pair_bias_weight, "first_operand_coeffs": first_operand_coeffs, "other_operand_coeffs": other_operand_coeffs, "outer_output_weight": outer_output_weight, "starting_projection_weight": starting_projection_weight, "starting_bias_weight": starting_bias_weight, "starting_output_weight": starting_output_weight, "ending_projection_weight": ending_projection_weight, "ending_bias_weight": ending_bias_weight, "ending_output_weight": ending_output_weight}


highest = lax.Precision.HIGHEST
epsilon = 1e-05
masked_score = -1000000000.0

def layer_normalize(values):
    centred = values - lax.optimization_barrier(jnp.mean(values, axis=-1, keepdims=True))
    variance = lax.optimization_barrier(jnp.mean(centred * centred, axis=-1, keepdims=True))
    return centred * lax.rsqrt(variance + epsilon)

def linear_project(values, weight):
    return jnp.dot(values, weight, precision=highest, preferred_element_type=jnp.float32)

def attend(query_matrix, key_matrix, value_matrix, gate_matrix, score_bias, live_keys, head_count):
    head_width = query_matrix.shape[-1] // head_count
    shaped_q = query_matrix.reshape(query_matrix.shape[0], head_count, head_width)
    shaped_k = key_matrix.reshape(key_matrix.shape[0], head_count, head_width)
    shaped_v = value_matrix.reshape(value_matrix.shape[0], head_count, head_width)
    scores = jnp.einsum('qhd,khd->hqk', shaped_q, shaped_k, precision=highest) / math.sqrt(head_width) + score_bias
    scores = jnp.where(live_keys[None, None, :], scores, masked_score)
    scores = scores - lax.optimization_barrier(jnp.max(scores, axis=-1, keepdims=True))
    weights = jnp.exp(scores)
    weights = weights / lax.optimization_barrier(jnp.sum(weights, axis=-1, keepdims=True))
    mixture = jnp.einsum('hqk,khd->qhd', weights, shaped_v, precision=highest)
    return jax.nn.sigmoid(gate_matrix) * mixture.reshape(query_matrix.shape[0], head_count * head_width)

def factor_matrix(normed, float_mask, weight):
    return jnp.transpose(linear_project(normed, weight) * float_mask[:, :, None], (1, 2, 0))

def outer_block(left_matrix, mask_rows, right_all, mask_all, out_weight):
    residues, factor_width, sequences = right_all.shape

    def one_row(operands):
        row_left, row_mask = operands
        outer_sum = jnp.einsum('cs,jes->jce', row_left, right_all, precision=highest)
        outer_sum = outer_sum.reshape(residues, factor_width * factor_width)
        intersection = jnp.einsum('ns,s->n', mask_all, row_mask, precision=highest)
        return linear_project(outer_sum, out_weight) / jnp.maximum(intersection, 1.0)[:, None]
    return lax.map(one_row, (left_matrix, mask_rows))

def starting_change(field, proj, bias_weight, out_weight, live_keys):
    normed = layer_normalize(field)
    score_bias = jnp.einsum('ijc,ch->hij', normed, bias_weight, precision=highest)
    query_matrix = linear_project(normed, proj[0])
    key_matrix = linear_project(normed, proj[1])
    value_matrix = linear_project(normed, proj[2])
    gate_matrix = linear_project(normed, proj[3])

    def one_row(operands):
        return attend(operands[0], operands[1], operands[2], operands[3], score_bias, live_keys, HEADS_Z)
    gated_output = lax.map(one_row, (query_matrix, key_matrix, value_matrix, gate_matrix))
    return linear_project(gated_output, out_weight)

def reference(alignment_representation, pairwise_state, alignment_mask, residue_present_mask, row_projection_weight, lateral_result_coeffs, pair_bias_weight, first_operand_coeffs, other_operand_coeffs, outer_output_weight, starting_projection_weight, starting_bias_weight, starting_output_weight, ending_projection_weight, ending_bias_weight, ending_output_weight):
    normed_alignment = layer_normalize(alignment_representation)
    row_bias = jnp.einsum('ijc,ch->hij', layer_normalize(pairwise_state), pair_bias_weight, precision=highest)
    query_matrix = linear_project(normed_alignment, row_projection_weight[0])
    key_matrix = linear_project(normed_alignment, row_projection_weight[1])
    value_matrix = linear_project(normed_alignment, row_projection_weight[2])
    gate_matrix = linear_project(normed_alignment, row_projection_weight[3])
    sequence_present = alignment_mask > 0

    def one_sequence(operands):
        return attend(operands[0], operands[1], operands[2], operands[3], row_bias, operands[4], ATTEND_HEADS)
    gated_output = lax.map(one_sequence, (query_matrix, key_matrix, value_matrix, gate_matrix, sequence_present))
    alignment_output = alignment_representation + linear_project(gated_output, lateral_result_coeffs)
    float_mask = alignment_mask.astype(jnp.float32)
    left_matrix = factor_matrix(normed_alignment, float_mask, first_operand_coeffs)
    right_matrix = factor_matrix(normed_alignment, float_mask, other_operand_coeffs)
    mask_rows = jnp.transpose(float_mask)
    update = outer_block(left_matrix, mask_rows, right_matrix, mask_rows, outer_output_weight)
    pair_one = pairwise_state + update
    live_keys = residue_present_mask > 0
    pairwise_second = pair_one + starting_change(pair_one, starting_projection_weight, starting_bias_weight, starting_output_weight, live_keys)
    flipped = jnp.transpose(pairwise_second, (1, 0, 2))
    ending = starting_change(flipped, ending_projection_weight, ending_bias_weight, ending_output_weight, live_keys)
    pairwise_output = pairwise_second + jnp.transpose(ending, (1, 0, 2))
    return (alignment_output, pairwise_output)
```

```python
import functools
import math

import jax
import jax.numpy as jnp
from jax import lax
from jax.experimental import pallas as pl
from jax.experimental.pallas import tpu as pltpu
from jax.sharding import PartitionSpec as P

epsilon = 1e-05
masked_score = -1000000000.0
EVERYONE = ("res", "branch")

NN = (((1,), (0,)), ((), ()))
NT = (((1,), (1,)), ((), ()))


def layer_normalize(values):
    centred = values - jnp.mean(values, axis=-1, keepdims=True)
    variance = jnp.mean(centred * centred, axis=-1, keepdims=True)
    return centred * lax.rsqrt(variance + epsilon)


def split(values):
    high = values.astype(jnp.bfloat16)
    return high, (values - high.astype(jnp.float32)).astype(jnp.bfloat16)


def dot3(a, b, dims=NN):
    (ah, al), (bh, bl) = a, b

    def one(x, y):
        return lax.dot_general(x, y, dims, preferred_element_type=jnp.float32)

    return one(ah, bh) + (one(ah, bl) + one(al, bh))


def attention_kernel(heads, x_ref, bias_ref, live_ref, proj_ref, out_w_ref, *rest):
    next_w_ref, o_ref, next_ref = rest if len(rest) == 3 else (None, rest[0], None)
    x = x_ref[0]
    channels = x.shape[1]
    width = channels // heads
    normed = split(layer_normalize(x))
    q, k, v, g = (dot3(normed, split(proj_ref[p])) for p in range(4))
    q = q * (1.0 / math.sqrt(width))
    keys = split(k)
    owner = lax.broadcasted_iota(jnp.int32, (1, channels), 1) // width
    live = live_ref[0] > 0.5
    mixture = None
    for h in range(heads):
        mine = owner == h
        scores = dot3(split(jnp.where(mine, q, 0.0)), keys, NT) + bias_ref[h]
        scores = jnp.where(live, scores, masked_score)
        weights = jnp.exp(scores - jnp.max(scores, axis=-1, keepdims=True))
        weights = weights / jnp.sum(weights, axis=-1, keepdims=True)
        term = dot3(split(weights), split(jnp.where(mine, v, 0.0)))
        mixture = term if mixture is None else mixture + term
    gated = jax.nn.sigmoid(g) * mixture
    result = x + dot3(split(gated), split(out_w_ref[...]))
    o_ref[0] = result
    if next_ref is not None:
        next_ref[0] = dot3(split(next_w_ref[...]), split(layer_normalize(result)), NT)


def attention(x, bias, live, proj, out_w, heads, next_w=None):
    lines, residues, channels = x.shape

    def whole(a):
        return pl.BlockSpec(a.shape, lambda i: (0,) * a.ndim)

    line = pl.BlockSpec((1, residues, channels), lambda i: (i, 0, 0))
    args = [x, bias, live, proj, out_w]
    in_specs = [
        line,
        whole(bias),
        pl.BlockSpec((1, 1, residues), lambda i: (i, 0, 0)),
        whole(proj),
        whole(out_w),
    ]
    out_shape = [jax.ShapeDtypeStruct(x.shape, jnp.float32)]
    out_specs = [line]
    if next_w is not None:
        args.append(next_w)
        in_specs.append(whole(next_w))
        out_shape.append(
            jax.ShapeDtypeStruct((lines, next_w.shape[0], residues), jnp.float32)
        )
        out_specs.append(
            pl.BlockSpec((1, next_w.shape[0], residues), lambda i: (i, 0, 0))
        )
    return pl.pallas_call(
        functools.partial(attention_kernel, heads),
        grid=(lines,),
        in_specs=in_specs,
        out_specs=out_specs,
        out_shape=out_shape,
    )(*args)


def outer_kernel(left_ref, right_ref, weight_ref, o_ref):
    rows, factors, sequences = left_ref.shape
    shares, half, padded, _ = right_ref.shape
    columns = shares * padded
    left = split(left_ref[...].reshape(rows * factors, sequences))
    weight = split(weight_ref[...])
    products = []
    for e in range(half):
        right = split(right_ref[:, e].reshape(columns, sequences))
        products.append(dot3(left, right, NT))
    for i in range(rows):
        block = jnp.concatenate(
            [one[i * factors : (i + 1) * factors] for one in products], axis=0
        )
        o_ref[i] = jnp.transpose(dot3(weight, split(block)))


def outer_product(left, right, weight):
    rows = left.shape[0]
    columns = right.shape[0] * right.shape[2]
    return pl.pallas_call(
        outer_kernel,
        out_shape=jax.ShapeDtypeStruct((rows, columns, weight.shape[0]), jnp.float32),
    )(left, right, weight)


def project(a, b, form):
    return jnp.einsum(form, a, b, precision=lax.Precision.HIGH)


def gather(block, axes, count):
    copies = jnp.broadcast_to(block[None], (count,) + block.shape)
    return lax.all_to_all(copies, axes, 0, 0)


def per_device(
    msa,
    pair,
    msa_mask,
    residue_mask,
    row_proj,
    row_out,
    row_bias_w,
    first_w,
    other_w,
    outer_w,
    start_proj,
    start_bias_w,
    start_out,
    end_proj,
    end_bias_w,
    end_out,
):
    b = lax.axis_index("branch")
    branches = lax.axis_size("branch")
    shares = lax.axis_size("res")
    everyone = branches * shares
    sequences, local, features = msa.shape
    residues, width = pair.shape[1:]
    factors = first_w.shape[1]
    half = factors // branches
    mine = local // branches
    per_seq = sequences // everyone
    padded = -(-local // 8) * 8

    depth = jnp.sum(msa_mask, axis=0).astype(jnp.float32)
    bias_rows = project(layer_normalize(pair), row_bias_w, "ijc,ch->ihj")
    bias_pack = jnp.concatenate(
        [bias_rows, jnp.broadcast_to(depth[:, None, None], (local, 1, residues))], axis=1
    )

    normed = layer_normalize(msa)
    my_other = lax.dynamic_slice_in_dim(other_w, b * half, half, axis=1)
    mask = jnp.transpose(msa_mask).astype(jnp.float32)
    left = project(normed, first_w, "sia,ac->ics") * mask[:, None, :]
    right = project(normed, my_other, "sja,ae->ejs") * mask[None]
    right = jnp.pad(right, ((0, 0), (0, padded - local), (0, 0)))
    right_all = gather(right, "res", shares)

    bias_all = gather(bias_pack, "res", shares).reshape(residues, -1, residues)
    row_bias = jnp.transpose(bias_all[:, :-1], (1, 0, 2))
    depth_all = bias_all[:, -1, 0]

    my_msa = lax.dynamic_slice_in_dim(msa, b * (sequences // branches), sequences // branches, axis=0)
    seq_msa = lax.all_to_all(my_msa, "res", split_axis=0, concat_axis=1, tiled=True)

    weight = outer_w.reshape(factors, factors, width)
    weight = lax.dynamic_slice_in_dim(weight, b * half, half, axis=1)
    weight = jnp.transpose(weight, (2, 1, 0)).reshape(width, half * factors)
    partial = outer_product(left, right_all, weight)
    partial = partial.reshape(branches, mine, shares, padded, width)[:, :, :, :local]
    partial = partial.reshape(branches, mine, residues, width)
    update = jnp.sum(lax.all_to_all(partial, "branch", 0, 0), axis=0)
    my_depth = lax.dynamic_slice_in_dim(depth, b * mine, mine)
    overlap = jnp.minimum(my_depth[:, None], depth_all[None])
    my_pair = lax.dynamic_slice_in_dim(pair, b * mine, mine)
    pair_one = my_pair + update / jnp.maximum(overlap, 1.0)[:, :, None]

    start_rows = project(layer_normalize(pair_one), start_bias_w, "ijc,ch->ihj")
    start_all = gather(start_rows, EVERYONE, everyone)
    heads_z = start_bias_w.shape[1]
    start_score = jnp.transpose(start_all.reshape(residues, heads_z, residues), (1, 0, 2))
    live = jnp.broadcast_to((depth_all > 0.5).astype(jnp.float32), (mine, 1, residues))
    next_w = jnp.pad(jnp.transpose(end_bias_w), ((0, -heads_z % 8), (0, 0)))
    pair_two, end_rows = attention(
        pair_one, start_score, live, start_proj, start_out, heads_z, next_w
    )
    end_all = gather(end_rows[:, :heads_z], EVERYONE, everyone)
    end_score = jnp.transpose(end_all.reshape(residues, heads_z, residues), (1, 2, 0))

    columns = lax.all_to_all(
        pair_two.reshape(mine, everyone, mine, width), EVERYONE, 1, 0
    )
    columns = jnp.transpose(columns.reshape(residues, mine, width), (1, 0, 2))

    start_of_seq = (b * shares + lax.axis_index("res")) * per_seq
    present = (
        start_of_seq + jnp.arange(per_seq)[:, None, None] < depth_all[None, None, :]
    ).astype(jnp.float32)
    (seq_result,) = attention(
        seq_msa, row_bias, present, row_proj, row_out, row_bias_w.shape[1]
    )
    msa_result = lax.all_to_all(seq_result, "res", split_axis=1, concat_axis=0, tiled=True)

    (end_result,) = attention(columns, end_score, live, end_proj, end_out, heads_z)
    tiles = end_result.reshape(mine, shares, local, branches, width // branches)
    tiles = jnp.transpose(tiles, (1, 3, 2, 0, 4)).reshape(
        everyone, local, mine, width // branches
    )
    pair_result = lax.all_to_all(tiles, EVERYONE, 0, 0)
    pair_result = jnp.transpose(pair_result, (1, 0, 2, 3)).reshape(
        local, residues, width // branches
    )
    return msa_result, pair_result


def solution(mesh):
    in_specs = (
        P(None, "res", None),
        P("res", None, None),
        P(None, "res"),
        P("res"),
    ) + (P(),) * 12
    out_specs = (P("branch", "res", None), P("res", None, "branch"))
    return jax.shard_map(
        per_device, mesh=mesh, in_specs=in_specs, out_specs=out_specs, check_vma=False
    )
```

```python
import functools
import math

import jax
import jax.numpy as jnp
from jax import lax
from jax.experimental import pallas as pl
from jax.experimental.pallas import tpu as pltpu
from jax.sharding import PartitionSpec as P

epsilon = 1e-05
masked_score = -1000000000.0
EVERYONE = ("res", "branch")

NN = (((1,), (0,)), ((), ()))
NT = (((1,), (1,)), ((), ()))


def layer_normalize(values):
    centred = values - jnp.mean(values, axis=-1, keepdims=True)
    variance = jnp.mean(centred * centred, axis=-1, keepdims=True)
    return centred * lax.rsqrt(variance + epsilon)


def split(values):
    high = values.astype(jnp.bfloat16)
    return high, (values - high.astype(jnp.float32)).astype(jnp.bfloat16)


def dot3(a, b, dims=NN):
    (ah, al), (bh, bl) = a, b

    def one(x, y):
        return lax.dot_general(x, y, dims, preferred_element_type=jnp.float32)

    return one(ah, bh) + (one(ah, bl) + one(al, bh))


def attention_kernel(heads, x_ref, bias_ref, live_ref, proj_ref, out_w_ref, *rest):
    next_w_ref, o_ref, next_ref = rest if len(rest) == 3 else (None, rest[0], None)
    x = x_ref[0]
    channels = x.shape[1]
    width = channels // heads
    normed = split(layer_normalize(x))
    q, k, v, g = (dot3(normed, split(proj_ref[p])) for p in range(4))
    q = q * (1.0 / math.sqrt(width))
    keys = split(k)
    owner = lax.broadcasted_iota(jnp.int32, (1, channels), 1) // width
    live = live_ref[0] > 0.5
    mixture = None
    for h in range(heads):
        mine = owner == h
        scores = dot3(split(jnp.where(mine, q, 0.0)), keys, NT) + bias_ref[h]
        scores = jnp.where(live, scores, masked_score)
        weights = jnp.exp(scores - jnp.max(scores, axis=-1, keepdims=True))
        weights = weights / jnp.sum(weights, axis=-1, keepdims=True)
        term = dot3(split(weights), split(jnp.where(mine, v, 0.0)))
        mixture = term if mixture is None else mixture + term
    gated = jax.nn.sigmoid(g) * mixture
    result = x + dot3(split(gated), split(out_w_ref[...]))
    o_ref[0] = result
    if next_ref is not None:
        next_ref[0] = dot3(split(next_w_ref[...]), split(layer_normalize(result)), NT)


def attention(x, bias, live, proj, out_w, heads, next_w=None):
    lines, residues, channels = x.shape

    def whole(a):
        return pl.BlockSpec(a.shape, lambda i: (0,) * a.ndim)

    line = pl.BlockSpec((1, residues, channels), lambda i: (i, 0, 0))
    args = [x, bias, live, proj, out_w]
    in_specs = [
        line,
        whole(bias),
        pl.BlockSpec((1, 1, residues), lambda i: (i, 0, 0)),
        whole(proj),
        whole(out_w),
    ]
    out_shape = [jax.ShapeDtypeStruct(x.shape, jnp.float32)]
    out_specs = [line]
    if next_w is not None:
        args.append(next_w)
        in_specs.append(whole(next_w))
        out_shape.append(
            jax.ShapeDtypeStruct((lines, next_w.shape[0], residues), jnp.float32)
        )
        out_specs.append(
            pl.BlockSpec((1, next_w.shape[0], residues), lambda i: (i, 0, 0))
        )
    return pl.pallas_call(
        functools.partial(attention_kernel, heads),
        grid=(lines,),
        in_specs=in_specs,
        out_specs=out_specs,
        out_shape=out_shape,
    )(*args)


def outer_kernel(left_ref, right_ref, weight_ref, o_ref):
    rows, factors, sequences = left_ref.shape
    shares, half, padded, _ = right_ref.shape
    columns = shares * padded
    left = split(left_ref[...].reshape(rows * factors, sequences))
    weight = split(weight_ref[...])
    products = []
    for e in range(half):
        right = split(right_ref[:, e].reshape(columns, sequences))
        products.append(dot3(left, right, NT))
    for i in range(rows):
        block = jnp.concatenate(
            [one[i * factors : (i + 1) * factors] for one in products], axis=0
        )
        o_ref[i] = jnp.transpose(dot3(weight, split(block)))


def outer_product(left, right, weight):
    rows = left.shape[0]
    columns = right.shape[0] * right.shape[2]
    return pl.pallas_call(
        outer_kernel,
        out_shape=jax.ShapeDtypeStruct((rows, columns, weight.shape[0]), jnp.float32),
    )(left, right, weight)


def project(a, b, form):
    return jnp.einsum(form, a, b, precision=lax.Precision.HIGH)


def gather(block, axes, count):
    copies = jnp.broadcast_to(block[None], (count,) + block.shape)
    return lax.all_to_all(copies, axes, 0, 0)


MESH = pl.DeviceIdType.MESH


def rows_attention(x, bias_of, mask_of, proj, out_w, heads):
    channels = x.shape[1]
    width = channels // heads
    normed = split(layer_normalize(x))
    q, k, v, g = (dot3(normed, split(proj[p])) for p in range(4))
    q = q * (1.0 / math.sqrt(width))
    keys = split(k)
    owner = lax.broadcasted_iota(jnp.int32, (1, channels), 1) // width
    mixture = None
    for h in range(heads):
        mine = owner == h
        scores = dot3(split(jnp.where(mine, q, 0.0)), keys, NT) + bias_of(h)
        scores = mask_of(scores)
        weights = jnp.exp(scores - jnp.max(scores, axis=-1, keepdims=True))
        weights = weights / jnp.sum(weights, axis=-1, keepdims=True)
        term = dot3(split(weights), split(jnp.where(mine, v, 0.0)))
        mixture = term if mixture is None else mixture + term
    return x + dot3(split(jax.nn.sigmoid(g) * mixture), split(out_w[...]))


def block_kernel(
    local,
    branches,
    shares,
    heads,
    heads_z,
    right_ref,
    left_ref,
    outer_ref,
    bias_ref,
    msa_ref,
    pair_ref,
    depth_ref,
    row_proj,
    row_out,
    start_proj,
    start_w,
    start_out,
    end_proj,
    end_w,
    end_out,
    msa_o,
    pair_o,
    right_all,
    bias_all,
    seq_in,
    seq_res,
    part_out,
    part_in,
    pair_one,
    start_send,
    start_all,
    tile_send,
    tile_all,
    column_in,
    pair_send,
    own_sem,
    ag_send,
    ag_recv,
    x_send,
    x_recv,
    c_send,
    c_recv,
    in_send,
    in_recv,
    out_send,
    out_recv,
    y_send,
    y_recv,
    s_send,
    s_recv,
    t_send,
    t_recv,
    p_send,
    p_recv,
):
    b = lax.axis_index("branch")
    r = lax.axis_index("res")
    everyone = branches * shares
    me = r * branches + b
    mine = local // branches
    per_seq = seq_in.shape[0]
    padded = right_ref.shape[1]
    residues = shares * padded
    factors = left_ref.shape[1]
    half = right_ref.shape[0]
    outers = shares // 4
    outer, inner = r // 4, r % 4
    twin_x = outer * 4 + (inner + 2) % 4
    twin_c = outer * 4 + (inner // 2) * 2 + (inner + 1) % 2
    my_rows = r * padded + b * mine

    def remote(src, dst, send, recv, branch, res):
        return pltpu.make_async_remote_copy(
            src_ref=src,
            dst_ref=dst,
            send_sem=send,
            recv_sem=recv,
            device_id={"branch": branch, "res": res},
            device_id_type=MESH,
        )

    def each(low, high, body):
        def step(k, carry):
            body(k)
            return carry

        lax.fori_loop(low, high, step, 0)

    start_all[...] = jnp.zeros_like(start_all)
    tile_all[...] = jnp.zeros_like(tile_all)

    barrier = pltpu.get_barrier_semaphore()

    def greet(k):
        other = (me + k) % everyone
        pl.semaphore_signal(
            barrier,
            inc=1,
            device_id={"branch": other % branches, "res": other // branches},
            device_id_type=MESH,
        )

    each(1, everyone, greet)
    pl.semaphore_wait(barrier, everyone - 1)

    pairs = ((right_ref, right_all, 0), (bias_ref, bias_all, 1))

    def stage_one(k, which):
        source, target, n = which
        peer = ((outer + k) % outers) * 4 + inner
        return remote(source, target.at[r], ag_send.at[n, k], ag_recv.at[n, k], b, peer)

    def stage_two(k, which):
        _, target, n = which
        at = ((outer + outers - k) % outers) * 4 + inner
        return remote(
            target.at[at], target.at[at], x_send.at[n, k], x_recv.at[n, k], b, twin_x
        )

    def stage_three(k, side, which):
        _, target, n = which
        at = ((outer + outers - k) % outers) * 4 + (inner + 2 * side) % 4
        return remote(
            target.at[at],
            target.at[at],
            c_send.at[n, side, k],
            c_recv.at[n, side, k],
            b,
            twin_c,
        )

    def seq_copy(k):
        peer = (r + k) % shares
        return remote(
            msa_ref.at[pl.ds(peer * per_seq, per_seq)],
            seq_in.at[:, r],
            in_send.at[k],
            in_recv.at[k],
            b,
            peer,
        )

    own = [
        pltpu.make_async_copy(right_ref, right_all.at[r], own_sem.at[0]),
        pltpu.make_async_copy(bias_ref, bias_all.at[r], own_sem.at[1]),
        pltpu.make_async_copy(
            msa_ref.at[pl.ds(r * per_seq, per_seq)], seq_in.at[:, r], own_sem.at[2]
        ),
    ]
    for copy in own:
        copy.start()
    for which in pairs:
        each(1, outers, lambda k: stage_one(k, which).start())
    for copy in own:
        copy.wait()
    for which in pairs:
        stage_two(0, which).start()
        stage_three(0, 0, which).start()
    each(1, shares, lambda k: seq_copy(k).start())
    for which in pairs:

        def forward(k):
            stage_one(k, which).wait()
            stage_two(k, which).start()
            stage_three(k, 0, which).start()

        each(1, outers, forward)
    for which in pairs:

        def forward_x(k):
            stage_two(k, which).wait()
            stage_three(k, 1, which).start()

        each(0, outers, forward_x)
    for which in pairs:

        def finish(k):
            stage_three(k, 0, which).wait()
            stage_three(k, 1, which).wait()

        each(0, outers, finish)

    other_b = (b + 1) % branches
    left = jnp.concatenate(
        [left_ref[pl.ds(other_b * mine, mine)], left_ref[pl.ds(b * mine, mine)]], axis=0
    ).reshape(local * factors, left_ref.shape[2])
    left = split(left)
    weight = split(outer_ref[...])
    products = []
    for e in range(half):
        right = split(right_all[:, e].reshape(residues, right_all.shape[3]))
        products.append(dot3(left, right, NT))

    def outer_row(i):
        block = jnp.concatenate(
            [one[i * factors : (i + 1) * factors] for one in products], axis=0
        )
        return jnp.transpose(dot3(weight, split(block)))

    for i in range(mine):
        part_out[i] = outer_row(i)
    swap = remote(part_out, part_in, y_send, y_recv, other_b, r)
    swap.start()
    for i in range(mine):
        pair_one[i] = outer_row(mine + i)

    depth = jnp.sum(bias_all[:, local, 0, :], axis=0, keepdims=True)
    depth_rows = jnp.transpose(jnp.broadcast_to(depth, (residues, residues)))
    lane = lax.broadcasted_iota(jnp.int32, (1, residues), 1)
    dead = jnp.where(lane % padded < local, masked_score, 3.0 * masked_score)
    present = depth > 0.5

    def pair_mask(scores):
        return jnp.where(present, scores, dead)

    first_seq = ((b * shares + r) * per_seq).astype(jnp.float32)

    def row_sequence(s):
        live = depth > first_seq + s.astype(jnp.float32)
        x = seq_in[s].reshape(residues, seq_in.shape[3])
        seq_res[s] = rows_attention(
            x,
            lambda h: bias_all[:, :, h, :].reshape(residues, residues),
            lambda scores: jnp.where(live, scores, dead),
            row_proj,
            row_out,
            heads,
        )

    swap.wait()
    for i in range(mine):
        update = pair_one[i] + part_in[i]
        overlap = jnp.maximum(jnp.minimum(depth_rows, depth_ref[i]), 1.0)
        pair_one[i] = pair_ref[i] + update / overlap
        start_send[i] = dot3(
            split(start_w[...]), split(layer_normalize(pair_one[i])), NT
        )[:heads_z]

    def start_copy(k):
        other = (me + k) % everyone
        return remote(
            start_send,
            start_all.at[pl.ds(my_rows, mine)],
            s_send.at[k],
            s_recv.at[k],
            other % branches,
            other // branches,
        )

    each(1, everyone, lambda k: start_copy(k).start())
    own = pltpu.make_async_copy(
        start_send, start_all.at[pl.ds(my_rows, mine)], own_sem.at[0]
    )
    own.start()

    each(1, shares, lambda k: seq_copy(k).wait())
    each(0, per_seq // 2, row_sequence)

    own.wait()
    each(1, everyone, lambda k: start_copy(k).wait())

    for i in range(mine):
        two = rows_attention(
            pair_one[i],
            lambda h: start_all[:, h, :],
            pair_mask,
            start_proj,
            start_out,
            heads_z,
        )
        rows = dot3(split(end_w[...]), split(layer_normalize(two)), NT)[:heads_z]
        for d in range(everyone):
            at = (d // branches) * padded + (d % branches) * mine
            tile_send[d, i, :mine] = two[at : at + mine]
            tile_send[d, i, mine : mine + heads_z] = rows

    def tile_copy(k):
        other = (me + k) % everyone
        return remote(
            tile_send.at[other],
            tile_all.at[pl.ds(my_rows, mine)],
            t_send.at[k],
            t_recv.at[k],
            other % branches,
            other // branches,
        )

    each(1, everyone, lambda k: tile_copy(k).start())
    own = pltpu.make_async_copy(
        tile_send.at[me], tile_all.at[pl.ds(my_rows, mine)], own_sem.at[0]
    )
    own.start()
    each(per_seq // 2, per_seq, row_sequence)

    def row_copy(k):
        peer = (r + k) % shares
        return remote(
            seq_res.at[:, pl.ds(pl.multiple_of(peer * padded, padded), padded), :],
            msa_o.at[pl.ds(r * per_seq, per_seq)],
            out_send.at[k],
            out_recv.at[k],
            b,
            peer,
        )

    own.wait()
    each(1, everyone, lambda k: tile_copy(k).wait())
    each(1, shares, lambda k: row_copy(k).start())
    own_row = pltpu.make_async_copy(
        seq_res.at[:, pl.ds(pl.multiple_of(r * padded, padded), padded), :],
        msa_o.at[pl.ds(r * per_seq, per_seq)],
        own_sem.at[1],
    )
    own_row.start()

    width = pair_ref.shape[2]
    share = width // branches
    for h in range(heads_z):
        column_in[h] = jnp.transpose(tile_all[:, mine + h, :])
    results = []
    for i in range(mine):
        results.append(
            rows_attention(
                tile_all[:, i, :],
                lambda h: column_in[h],
                pair_mask,
                end_proj,
                end_out,
                heads_z,
            )
        )
    for c in range(branches):
        pair_send[c] = jnp.concatenate(
            [one[:, c * share : (c + 1) * share] for one in results]
            + [jnp.zeros((residues, pair_send.shape[2] - mine * share), jnp.float32)],
            axis=1,
        )

    def pair_copy(k):
        other = (me + k) % everyone
        at = pl.multiple_of((other // branches) * padded, padded)
        return remote(
            pair_send.at[other % branches, pl.ds(at, padded), :],
            pair_o.at[me],
            p_send.at[k],
            p_recv.at[k],
            other % branches,
            other // branches,
        )

    each(1, everyone, lambda k: pair_copy(k).start())
    own = pltpu.make_async_copy(
        pair_send.at[b, pl.ds(pl.multiple_of(r * padded, padded), padded), :],
        pair_o.at[me],
        own_sem.at[0],
    )
    own.start()
    own.wait()
    own_row.wait()
    each(1, shares, lambda k: row_copy(k).wait())
    each(1, everyone, lambda k: pair_copy(k).wait())


def fused(
    msa, pair, msa_mask, row_proj, row_out, row_bias_w, first_w, other_w, outer_w,
    start_proj, start_bias_w, start_out, end_proj, end_bias_w, end_out, padded,
):
    b = lax.axis_index("branch")
    r = lax.axis_index("res")
    branches = lax.axis_size("branch")
    shares = lax.axis_size("res")
    everyone = branches * shares
    sequences, local, features = msa.shape
    residues, width = pair.shape[1:]
    factors = first_w.shape[1]
    half = factors // branches
    mine = local // branches
    per_seq = sequences // everyone
    spread = shares * padded
    heads, heads_z = row_bias_w.shape[1], start_bias_w.shape[1]
    spare = padded - local

    depth = jnp.sum(msa_mask, axis=0).astype(jnp.float32)
    wide = jnp.pad(
        pair.reshape(local, shares, local, width), ((0, 0), (0, 0), (0, spare), (0, 0))
    ).reshape(local, spread, width)
    bias_rows = project(layer_normalize(wide), row_bias_w, "ijc,ch->ihj")
    placed = lax.dynamic_update_slice(jnp.zeros((spread,), jnp.float32), depth, (r * padded,))
    bias_pack = jnp.concatenate(
        [bias_rows, jnp.broadcast_to(placed, (spare, heads, spread))], axis=0
    )
    normed = layer_normalize(msa)
    my_other = lax.dynamic_slice_in_dim(other_w, b * half, half, axis=1)
    mask = jnp.transpose(msa_mask).astype(jnp.float32)
    left = project(normed, first_w, "sia,ac->ics") * mask[:, None, :]
    right = project(normed, my_other, "sja,ae->ejs") * mask[None]
    right = jnp.pad(right, ((0, 0), (0, spare), (0, 0)))
    part = sequences // branches
    my_msa = lax.dynamic_slice_in_dim(msa, b * part, part, axis=0)
    my_msa = jnp.pad(my_msa, ((0, 0), (0, spare), (0, 0)))
    weight = outer_w.reshape(factors, factors, width)
    weight = lax.dynamic_slice_in_dim(weight, b * half, half, axis=1)
    weight = jnp.transpose(weight, (2, 1, 0)).reshape(width, half * factors)
    my_pair = lax.dynamic_slice_in_dim(wide, b * mine, mine)
    my_depth = lax.dynamic_slice_in_dim(depth, b * mine, mine)
    my_depth = jnp.broadcast_to(my_depth[:, None, None], (mine, 1, width))
    start_w = jnp.pad(jnp.transpose(start_bias_w), ((0, -heads_z % 8), (0, 0)))
    end_w = jnp.pad(jnp.transpose(end_bias_w), ((0, -heads_z % 8), (0, 0)))

    outers = shares // 4
    lanes = -(-(mine * (width // branches)) // 128) * 128
    stack = -(-(mine + heads_z) // 8) * 8
    f32 = jnp.float32
    dma = pltpu.SemaphoreType.DMA
    vmem = pl.BlockSpec(memory_space=pltpu.VMEM)
    args = (
        right, left, weight, bias_pack, my_msa, my_pair, my_depth, row_proj, row_out,
        start_proj, start_w, start_out, end_proj, end_w, end_out,
    )
    msa_o, pair_o = pl.pallas_call(
        functools.partial(block_kernel, local, branches, shares, heads, heads_z),
        out_shape=(
            jax.ShapeDtypeStruct((part, padded, features), f32),
            jax.ShapeDtypeStruct((everyone, padded, lanes), f32),
        ),
        in_specs=[vmem] * len(args),
        out_specs=(vmem, vmem),
        scratch_shapes=[
            pltpu.VMEM((shares,) + right.shape, f32),
            pltpu.VMEM((shares,) + bias_pack.shape, f32),
            pltpu.VMEM((per_seq, shares, padded, features), f32),
            pltpu.VMEM((per_seq, spread, features), f32),
            pltpu.VMEM((mine, spread, width), f32),
            pltpu.VMEM((mine, spread, width), f32),
            pltpu.VMEM((mine, spread, width), f32),
            pltpu.VMEM((mine, heads_z, spread), f32),
            pltpu.VMEM((spread, heads_z, spread), f32),
            pltpu.VMEM((everyone, mine, stack, width), f32),
            pltpu.VMEM((spread, stack, width), f32),
            pltpu.VMEM((heads_z, spread, spread), f32),
            pltpu.VMEM((branches, spread, lanes), f32),
            dma((3,)),
            dma((2, outers)),
            dma((2, outers)),
            dma((2, outers)),
            dma((2, outers)),
            dma((2, 2, outers)),
            dma((2, 2, outers)),
            dma((shares,)),
            dma((shares,)),
            dma((shares,)),
            dma((shares,)),
            dma,
            dma,
            dma((everyone,)),
            dma((everyone,)),
            dma((everyone,)),
            dma((everyone,)),
            dma((everyone,)),
            dma((everyone,)),
        ],
        compiler_params=pltpu.CompilerParams(
            collective_id=0, has_side_effects=True, vmem_limit_bytes=56 * 1024 * 1024
        ),
    )(*args)
    piece = width // branches
    pair_o = pair_o[:, :local, : mine * piece].reshape(everyone, local, mine, piece)
    pair_o = jnp.transpose(pair_o, (1, 0, 2, 3)).reshape(local, residues, piece)
    return msa_o[:, :local], pair_o


def per_device(
    msa,
    pair,
    msa_mask,
    residue_mask,
    row_proj,
    row_out,
    row_bias_w,
    first_w,
    other_w,
    outer_w,
    start_proj,
    start_bias_w,
    start_out,
    end_proj,
    end_bias_w,
    end_out,
):
    b = lax.axis_index("branch")
    branches = lax.axis_size("branch")
    shares = lax.axis_size("res")
    everyone = branches * shares
    sequences, local, features = msa.shape
    residues, width = pair.shape[1:]
    factors = first_w.shape[1]
    half = factors // branches
    mine = local // branches
    per_seq = sequences // everyone
    room = -(-(local + 1) // 8) * 8
    if shares * room == width and shares % 4 == 0 and width == 128:
        return fused(
            msa, pair, msa_mask, row_proj, row_out, row_bias_w, first_w, other_w, outer_w,
            start_proj, start_bias_w, start_out, end_proj, end_bias_w, end_out, room,
        )
    padded = -(-local // 8) * 8

    depth = jnp.sum(msa_mask, axis=0).astype(jnp.float32)
    bias_rows = project(layer_normalize(pair), row_bias_w, "ijc,ch->ihj")
    bias_pack = jnp.concatenate(
        [bias_rows, jnp.broadcast_to(depth[:, None, None], (local, 1, residues))], axis=1
    )

    normed = layer_normalize(msa)
    my_other = lax.dynamic_slice_in_dim(other_w, b * half, half, axis=1)
    mask = jnp.transpose(msa_mask).astype(jnp.float32)
    left = project(normed, first_w, "sia,ac->ics") * mask[:, None, :]
    right = project(normed, my_other, "sja,ae->ejs") * mask[None]
    right = jnp.pad(right, ((0, 0), (0, padded - local), (0, 0)))
    right_all = gather(right, "res", shares)

    bias_all = gather(bias_pack, "res", shares).reshape(residues, -1, residues)
    row_bias = jnp.transpose(bias_all[:, :-1], (1, 0, 2))
    depth_all = bias_all[:, -1, 0]

    my_msa = lax.dynamic_slice_in_dim(msa, b * (sequences // branches), sequences // branches, axis=0)
    seq_msa = lax.all_to_all(my_msa, "res", split_axis=0, concat_axis=1, tiled=True)

    weight = outer_w.reshape(factors, factors, width)
    weight = lax.dynamic_slice_in_dim(weight, b * half, half, axis=1)
    weight = jnp.transpose(weight, (2, 1, 0)).reshape(width, half * factors)
    partial = outer_product(left, right_all, weight)
    partial = partial.reshape(branches, mine, shares, padded, width)[:, :, :, :local]
    partial = partial.reshape(branches, mine, residues, width)
    update = jnp.sum(lax.all_to_all(partial, "branch", 0, 0), axis=0)
    my_depth = lax.dynamic_slice_in_dim(depth, b * mine, mine)
    overlap = jnp.minimum(my_depth[:, None], depth_all[None])
    my_pair = lax.dynamic_slice_in_dim(pair, b * mine, mine)
    pair_one = my_pair + update / jnp.maximum(overlap, 1.0)[:, :, None]

    start_rows = project(layer_normalize(pair_one), start_bias_w, "ijc,ch->ihj")
    start_all = gather(start_rows, EVERYONE, everyone)
    heads_z = start_bias_w.shape[1]
    start_score = jnp.transpose(start_all.reshape(residues, heads_z, residues), (1, 0, 2))
    live = jnp.broadcast_to((depth_all > 0.5).astype(jnp.float32), (mine, 1, residues))
    next_w = jnp.pad(jnp.transpose(end_bias_w), ((0, -heads_z % 8), (0, 0)))
    pair_two, end_rows = attention(
        pair_one, start_score, live, start_proj, start_out, heads_z, next_w
    )
    end_all = gather(end_rows[:, :heads_z], EVERYONE, everyone)
    end_score = jnp.transpose(end_all.reshape(residues, heads_z, residues), (1, 2, 0))

    columns = lax.all_to_all(
        pair_two.reshape(mine, everyone, mine, width), EVERYONE, 1, 0
    )
    columns = jnp.transpose(columns.reshape(residues, mine, width), (1, 0, 2))

    start_of_seq = (b * shares + lax.axis_index("res")) * per_seq
    present = (
        start_of_seq + jnp.arange(per_seq)[:, None, None] < depth_all[None, None, :]
    ).astype(jnp.float32)
    (seq_result,) = attention(
        seq_msa, row_bias, present, row_proj, row_out, row_bias_w.shape[1]
    )
    msa_result = lax.all_to_all(seq_result, "res", split_axis=1, concat_axis=0, tiled=True)

    (end_result,) = attention(columns, end_score, live, end_proj, end_out, heads_z)
    tiles = end_result.reshape(mine, shares, local, branches, width // branches)
    tiles = jnp.transpose(tiles, (1, 3, 2, 0, 4)).reshape(
        everyone, local, mine, width // branches
    )
    pair_result = lax.all_to_all(tiles, EVERYONE, 0, 0)
    pair_result = jnp.transpose(pair_result, (1, 0, 2, 3)).reshape(
        local, residues, width // branches
    )
    return msa_result, pair_result


def solution(mesh):
    in_specs = (
        P(None, "res", None),
        P("res", None, None),
        P(None, "res"),
        P("res"),
    ) + (P(),) * 12
    out_specs = (P("branch", "res", None), P("res", None, "branch"))
    return jax.shard_map(
        per_device, mesh=mesh, in_specs=in_specs, out_specs=out_specs, check_vma=False
    )
```

```python
import functools
import math

import jax
import jax.numpy as jnp
from jax import lax
from jax.experimental import pallas as pl
from jax.experimental.pallas import tpu as pltpu
from jax.sharding import PartitionSpec as P

epsilon = 1e-05
masked_score = -1000000000.0
EVERYONE = ("res", "branch")

NN = (((1,), (0,)), ((), ()))
NT = (((1,), (1,)), ((), ()))


def layer_normalize(values):
    centred = values - jnp.mean(values, axis=-1, keepdims=True)
    variance = jnp.mean(centred * centred, axis=-1, keepdims=True)
    return centred * lax.rsqrt(variance + epsilon)


def split(values):
    high = values.astype(jnp.bfloat16)
    return high, (values - high.astype(jnp.float32)).astype(jnp.bfloat16)


def dot3(a, b, dims=NN):
    (ah, al), (bh, bl) = a, b

    def one(x, y):
        return lax.dot_general(x, y, dims, preferred_element_type=jnp.float32)

    return one(ah, bh) + (one(ah, bl) + one(al, bh))


def attention_kernel(heads, x_ref, bias_ref, live_ref, proj_ref, out_w_ref, *rest):
    next_w_ref, o_ref, next_ref = rest if len(rest) == 3 else (None, rest[0], None)
    x = x_ref[0]
    channels = x.shape[1]
    width = channels // heads
    normed = split(layer_normalize(x))
    q, k, v, g = (dot3(normed, split(proj_ref[p])) for p in range(4))
    q = q * (1.0 / math.sqrt(width))
    keys = split(k)
    owner = lax.broadcasted_iota(jnp.int32, (1, channels), 1) // width
    live = live_ref[0] > 0.5
    mixture = None
    for h in range(heads):
        mine = owner == h
        scores = dot3(split(jnp.where(mine, q, 0.0)), keys, NT) + bias_ref[h]
        scores = jnp.where(live, scores, masked_score)
        weights = jnp.exp(scores - jnp.max(scores, axis=-1, keepdims=True))
        weights = weights / jnp.sum(weights, axis=-1, keepdims=True)
        term = dot3(split(weights), split(jnp.where(mine, v, 0.0)))
        mixture = term if mixture is None else mixture + term
    gated = jax.nn.sigmoid(g) * mixture
    result = x + dot3(split(gated), split(out_w_ref[...]))
    o_ref[0] = result
    if next_ref is not None:
        next_ref[0] = dot3(split(next_w_ref[...]), split(layer_normalize(result)), NT)


def attention(x, bias, live, proj, out_w, heads, next_w=None):
    lines, residues, channels = x.shape

    def whole(a):
        return pl.BlockSpec(a.shape, lambda i: (0,) * a.ndim)

    line = pl.BlockSpec((1, residues, channels), lambda i: (i, 0, 0))
    args = [x, bias, live, proj, out_w]
    in_specs = [
        line,
        whole(bias),
        pl.BlockSpec((1, 1, residues), lambda i: (i, 0, 0)),
        whole(proj),
        whole(out_w),
    ]
    out_shape = [jax.ShapeDtypeStruct(x.shape, jnp.float32)]
    out_specs = [line]
    if next_w is not None:
        args.append(next_w)
        in_specs.append(whole(next_w))
        out_shape.append(
            jax.ShapeDtypeStruct((lines, next_w.shape[0], residues), jnp.float32)
        )
        out_specs.append(
            pl.BlockSpec((1, next_w.shape[0], residues), lambda i: (i, 0, 0))
        )
    return pl.pallas_call(
        functools.partial(attention_kernel, heads),
        grid=(lines,),
        in_specs=in_specs,
        out_specs=out_specs,
        out_shape=out_shape,
    )(*args)


def outer_kernel(left_ref, right_ref, weight_ref, o_ref):
    rows, factors, sequences = left_ref.shape
    shares, half, padded, _ = right_ref.shape
    columns = shares * padded
    left = split(left_ref[...].reshape(rows * factors, sequences))
    weight = split(weight_ref[...])
    products = []
    for e in range(half):
        right = split(right_ref[:, e].reshape(columns, sequences))
        products.append(dot3(left, right, NT))
    for i in range(rows):
        block = jnp.concatenate(
            [one[i * factors : (i + 1) * factors] for one in products], axis=0
        )
        o_ref[i] = jnp.transpose(dot3(weight, split(block)))


def outer_product(left, right, weight):
    rows = left.shape[0]
    columns = right.shape[0] * right.shape[2]
    return pl.pallas_call(
        outer_kernel,
        out_shape=jax.ShapeDtypeStruct((rows, columns, weight.shape[0]), jnp.float32),
    )(left, right, weight)


def project(a, b, form):
    return jnp.einsum(form, a, b, precision=lax.Precision.HIGH)


def gather(block, axes, count):
    copies = jnp.broadcast_to(block[None], (count,) + block.shape)
    return lax.all_to_all(copies, axes, 0, 0)


MESH = pl.DeviceIdType.MESH


def rows_attention(x, bias_of, mask_of, proj, out_w, heads):
    lines, channels = x.shape
    width = channels // heads
    tile = 128
    per_tile = tile // width
    normed = split(layer_normalize(x))
    q, k, v, g = (dot3(normed, split(proj[p])) for p in range(4))
    q = q * (1.0 / math.sqrt(width))
    owner = lax.broadcasted_iota(jnp.int32, (1, tile), 1) // width
    bf16 = jnp.bfloat16
    mixtures = []
    for first in range(0, channels, tile):

        def halves(values):
            values = values[:, first : first + tile]
            high = values.astype(bf16).astype(jnp.float32)
            return high, values - high

        (q_hi, q_lo), (k_hi, k_lo), (v_hi, v_lo) = halves(q), halves(k), halves(v)
        q_turn = pltpu.roll(q_hi, width, 1)
        k_turn = pltpu.roll(k_lo, width, 1)
        keys = [
            jnp.concatenate(
                [k_hi, jnp.where(owner % 2 == parity, k_hi, k_turn)], axis=1
            ).astype(bf16)
            for parity in range(2)
        ]
        total = None
        for n in range(per_tile):
            mine, after = owner == n, owner == (n + 1) % per_tile
            query = jnp.concatenate(
                [
                    jnp.where(mine, q_hi, 0.0),
                    jnp.where(mine, q_lo, jnp.where(after, q_turn, 0.0)),
                ],
                axis=1,
            ).astype(bf16)
            scores = lax.dot_general(
                query, keys[n % 2], NT, preferred_element_type=jnp.float32
            )
            scores = mask_of(scores + bias_of(first // width + n))
            weights = jnp.exp(scores - jnp.max(scores, axis=-1, keepdims=True))
            weights = weights / jnp.sum(weights, axis=-1, keepdims=True)
            w_hi, w_lo = split(weights)
            m_hi = jnp.where(mine, v_hi, 0.0).astype(bf16)
            m_lo = jnp.where(mine, v_lo, 0.0).astype(bf16)
            values = jnp.concatenate(
                [
                    jnp.concatenate([m_hi, m_lo], axis=1),
                    jnp.concatenate([m_hi, jnp.zeros_like(m_lo)], axis=1),
                ],
                axis=0,
            )
            term = lax.dot_general(
                jnp.concatenate([w_hi, w_lo], axis=1),
                values,
                NN,
                preferred_element_type=jnp.float32,
            )
            total = term if total is None else total + term
        mixtures.append(total[:, :tile] + total[:, tile:])
    mixture = mixtures[0] if len(mixtures) == 1 else jnp.concatenate(mixtures, axis=1)
    return x + dot3(split(jax.nn.sigmoid(g) * mixture), split(out_w[...]))


def block_kernel(
    local,
    branches,
    shares,
    heads,
    heads_z,
    msa_ref,
    mask_ref,
    wide_ref,
    place_ref,
    factor_w,
    bias_w,
    outer_ref,
    row_proj,
    row_out,
    start_proj,
    start_w,
    start_out,
    end_proj,
    end_w,
    end_out,
    msa_o,
    pair_o,
    left_ref,
    right_ref,
    bias_ref,
    pair_ref,
    seq_pad,
    right_all,
    bias_all,
    seq_in,
    seq_res,
    part_out,
    part_in,
    pair_one,
    start_send,
    start_all,
    tile_send,
    tile_all,
    column_in,
    pair_send,
    own_sem,
    ag_send,
    ag_recv,
    x_send,
    x_recv,
    c_send,
    c_recv,
    in_send,
    in_recv,
    out_send,
    out_recv,
    y_send,
    y_recv,
    s_send,
    s_recv,
    t_send,
    t_recv,
    p_send,
    p_recv,
):
    b = lax.axis_index("branch")
    r = lax.axis_index("res")
    everyone = branches * shares
    me = r * branches + b
    mine = local // branches
    per_seq = seq_in.shape[0]
    padded = right_ref.shape[1]
    residues = shares * padded
    factors = left_ref.shape[1]
    half = right_ref.shape[0]
    outers = shares // 4
    outer, inner = r // 4, r % 4
    twin_x = outer * 4 + (inner + 2) % 4
    twin_c = outer * 4 + (inner // 2) * 2 + (inner + 1) % 2
    my_rows = r * padded + b * mine

    def remote(src, dst, send, recv, branch, res):
        return pltpu.make_async_remote_copy(
            src_ref=src,
            dst_ref=dst,
            send_sem=send,
            recv_sem=recv,
            device_id={"branch": branch, "res": res},
            device_id_type=MESH,
        )

    def each(low, high, body):
        def step(k, carry):
            body(k)
            return carry

        lax.fori_loop(low, high, step, 0)

    start_all[...] = jnp.zeros_like(start_all)
    tile_all[...] = jnp.zeros_like(tile_all)
    right_ref[...] = jnp.zeros_like(right_ref)
    bias_ref[...] = jnp.zeros_like(bias_ref)
    seq_pad[...] = jnp.zeros_like(seq_pad)
    pair_ref[...] = jnp.zeros_like(pair_ref)

    barrier = pltpu.get_barrier_semaphore()

    def greet(k):
        other = (me + k) % everyone
        pl.semaphore_signal(
            barrier,
            inc=1,
            device_id={"branch": other % branches, "res": other // branches},
            device_id_type=MESH,
        )

    each(1, everyone, greet)

    factor = split(factor_w[...])
    for j in range(local):
        line = split(layer_normalize(msa_ref[:, j, :]))
        both = dot3(factor, line, NT) * mask_ref[j : j + 1]
        left_ref[j] = both[:factors]
        right_ref[:, j, :] = both[factors:]
    for i in range(local):
        for share in range(shares):
            pair_ref[i, share * padded : share * padded + local, :] = wide_ref[
                i, share * local : (share + 1) * local, :
            ]
    weight = split(bias_w[...])
    for i in range(local):
        bias_ref[i] = dot3(weight, split(layer_normalize(pair_ref[i])), NT)
    bias_ref[local] = jnp.broadcast_to(place_ref[...], bias_ref.shape[1:])
    pl.semaphore_wait(barrier, everyone - 1)

    pairs = ((right_ref, right_all, 0), (bias_ref, bias_all, 1))

    def stage_one(k, which):
        source, target, n = which
        peer = ((outer + k) % outers) * 4 + inner
        return remote(source, target.at[r], ag_send.at[n, k], ag_recv.at[n, k], b, peer)

    def stage_two(k, which):
        _, target, n = which
        at = ((outer + outers - k) % outers) * 4 + inner
        return remote(
            target.at[at], target.at[at], x_send.at[n, k], x_recv.at[n, k], b, twin_x
        )

    def stage_three(k, side, which):
        _, target, n = which
        at = ((outer + outers - k) % outers) * 4 + (inner + 2 * side) % 4
        return remote(
            target.at[at],
            target.at[at],
            c_send.at[n, side, k],
            c_recv.at[n, side, k],
            b,
            twin_c,
        )

    def seq_copy(k):
        peer = (r + k) % shares
        return remote(
            msa_ref.at[pl.ds((b * shares + peer) * per_seq, per_seq)],
            seq_in.at[:, r],
            in_send.at[k],
            in_recv.at[k],
            b,
            peer,
        )

    own = [
        pltpu.make_async_copy(right_ref, right_all.at[r], own_sem.at[0]),
        pltpu.make_async_copy(bias_ref, bias_all.at[r], own_sem.at[1]),
        pltpu.make_async_copy(
            msa_ref.at[pl.ds((b * shares + r) * per_seq, per_seq)], seq_in.at[:, r], own_sem.at[2]
        ),
    ]
    for copy in own:
        copy.start()
    for which in pairs:
        each(1, outers, lambda k: stage_one(k, which).start())
    for copy in own:
        copy.wait()
    for which in pairs:
        stage_two(0, which).start()
        stage_three(0, 0, which).start()
    each(1, shares, lambda k: seq_copy(k).start())
    for which in pairs:

        def forward(k):
            stage_one(k, which).wait()
            stage_two(k, which).start()
            stage_three(k, 0, which).start()

        each(1, outers, forward)
    for which in pairs:

        def forward_x(k):
            stage_two(k, which).wait()
            stage_three(k, 1, which).start()

        each(0, outers, forward_x)
    for which in pairs:

        def finish(k):
            stage_three(k, 0, which).wait()
            stage_three(k, 1, which).wait()

        each(0, outers, finish)

    other_b = (b + 1) % branches
    left = jnp.concatenate(
        [left_ref[pl.ds(other_b * mine, mine)], left_ref[pl.ds(b * mine, mine)]], axis=0
    ).reshape(local * factors, left_ref.shape[2])
    left = split(left)
    weight = split(outer_ref[...])
    products = []
    for e in range(half):
        right = split(right_all[:, e].reshape(residues, right_all.shape[3]))
        products.append(dot3(left, right, NT))

    def outer_row(i):
        block = jnp.concatenate(
            [one[i * factors : (i + 1) * factors] for one in products], axis=0
        )
        return jnp.transpose(dot3(weight, split(block)))

    for i in range(mine):
        part_out[i] = outer_row(i)
    swap = remote(part_out, part_in, y_send, y_recv, other_b, r)
    swap.start()
    for i in range(mine):
        pair_one[i] = outer_row(mine + i)

    depth = jnp.sum(bias_all[:, local, 0, :], axis=0, keepdims=True)
    depth_rows = jnp.transpose(jnp.broadcast_to(depth, (residues, residues)))
    lane = lax.broadcasted_iota(jnp.int32, (1, residues), 1)
    dead = jnp.where(lane % padded < local, masked_score, 3.0 * masked_score)
    present = depth > 0.5

    def pair_mask(scores):
        return jnp.where(present, scores, dead)

    first_seq = ((b * shares + r) * per_seq).astype(jnp.float32)

    def row_sequence(s):
        live = depth > first_seq + s.astype(jnp.float32)
        seq_pad[:, :local, :] = seq_in[s]
        x = seq_pad[...].reshape(residues, seq_in.shape[3])
        seq_res[s] = rows_attention(
            x,
            lambda h: bias_all[:, :, h, :].reshape(residues, residues),
            lambda scores: jnp.where(live, scores, dead),
            row_proj,
            row_out,
            heads,
        )

    column_in[0] = depth_rows
    swap.wait()
    for i in range(mine):
        update = pair_one[i] + part_in[i]
        overlap = jnp.maximum(jnp.minimum(depth_rows, column_in[0, pl.ds(my_rows + i, 1), :]), 1.0)
        pair_one[i] = pair_ref[b * mine + i] + update / overlap
        start_send[i] = dot3(
            split(start_w[...]), split(layer_normalize(pair_one[i])), NT
        )

    def start_copy(k):
        other = (me + k) % everyone
        return remote(
            start_send,
            start_all.at[pl.ds(my_rows, mine)],
            s_send.at[k],
            s_recv.at[k],
            other % branches,
            other // branches,
        )

    each(1, everyone, lambda k: start_copy(k).start())
    own = pltpu.make_async_copy(
        start_send, start_all.at[pl.ds(my_rows, mine)], own_sem.at[0]
    )
    own.start()

    each(1, shares, lambda k: seq_copy(k).wait())
    each(0, per_seq // 2, row_sequence)

    own.wait()
    each(1, everyone, lambda k: start_copy(k).wait())

    for i in range(mine):
        two = rows_attention(
            pair_one[i],
            lambda h: start_all[:, h, :],
            pair_mask,
            start_proj,
            start_out,
            heads_z,
        )
        rows = dot3(split(end_w[...]), split(layer_normalize(two)), NT)
        for d in range(everyone):
            at = (d // branches) * padded + (d % branches) * mine
            tile_send[d, i, :mine] = two[at : at + mine]
            tile_send[d, i, mine : mine + heads_z] = rows

    def tile_copy(k):
        other = (me + k) % everyone
        return remote(
            tile_send.at[other],
            tile_all.at[pl.ds(my_rows, mine)],
            t_send.at[k],
            t_recv.at[k],
            other % branches,
            other // branches,
        )

    each(1, everyone, lambda k: tile_copy(k).start())
    own = pltpu.make_async_copy(
        tile_send.at[me], tile_all.at[pl.ds(my_rows, mine)], own_sem.at[0]
    )
    own.start()
    each(per_seq // 2, per_seq, row_sequence)

    def row_copy(k):
        peer = (r + k) % shares
        return remote(
            seq_res.at[:, pl.ds(pl.multiple_of(peer * padded, padded), padded), :],
            msa_o.at[pl.ds(r * per_seq, per_seq)],
            out_send.at[k],
            out_recv.at[k],
            b,
            peer,
        )

    own.wait()
    each(1, everyone, lambda k: tile_copy(k).wait())
    each(1, shares, lambda k: row_copy(k).start())
    own_row = pltpu.make_async_copy(
        seq_res.at[:, pl.ds(pl.multiple_of(r * padded, padded), padded), :],
        msa_o.at[pl.ds(r * per_seq, per_seq)],
        own_sem.at[1],
    )
    own_row.start()

    width = pair_ref.shape[2]
    share = width // branches
    for h in range(heads_z):
        column_in[h] = jnp.transpose(tile_all[:, mine + h, :])
    results = []
    for i in range(mine):
        results.append(
            rows_attention(
                tile_all[:, i, :],
                lambda h: column_in[h],
                pair_mask,
                end_proj,
                end_out,
                heads_z,
            )
        )
    for c in range(branches):
        pair_send[c] = jnp.concatenate(
            [one[:, c * share : (c + 1) * share] for one in results]
            + [jnp.zeros((residues, pair_send.shape[2] - mine * share), jnp.float32)],
            axis=1,
        )

    def pair_copy(k):
        other = (me + k) % everyone
        at = pl.multiple_of((other // branches) * padded, padded)
        return remote(
            pair_send.at[other % branches, pl.ds(at, padded), :],
            pair_o.at[me],
            p_send.at[k],
            p_recv.at[k],
            other % branches,
            other // branches,
        )

    each(1, everyone, lambda k: pair_copy(k).start())
    own = pltpu.make_async_copy(
        pair_send.at[b, pl.ds(pl.multiple_of(r * padded, padded), padded), :],
        pair_o.at[me],
        own_sem.at[0],
    )
    own.start()
    own.wait()
    own_row.wait()
    each(1, shares, lambda k: row_copy(k).wait())
    each(1, everyone, lambda k: pair_copy(k).wait())


def fused(
    msa, pair, msa_mask, row_proj, row_out, row_bias_w, first_w, other_w, outer_w,
    start_proj, start_bias_w, start_out, end_proj, end_bias_w, end_out, padded,
):
    b = lax.axis_index("branch")
    r = lax.axis_index("res")
    branches = lax.axis_size("branch")
    shares = lax.axis_size("res")
    everyone = branches * shares
    sequences, local, features = msa.shape
    residues, width = pair.shape[1:]
    factors = first_w.shape[1]
    half = factors // branches
    mine = local // branches
    per_seq = sequences // everyone
    spread = shares * padded
    heads, heads_z = row_bias_w.shape[1], start_bias_w.shape[1]

    mask = jnp.transpose(msa_mask).astype(jnp.float32)
    depth = jnp.sum(mask, axis=1)
    place = lax.dynamic_update_slice(
        jnp.zeros((1, spread), jnp.float32), depth[None], (0, r * padded)
    )
    my_other = lax.dynamic_slice_in_dim(other_w, b * half, half, axis=1)
    factor_w = jnp.transpose(jnp.concatenate([first_w, my_other], axis=1))
    part = sequences // branches
    weight = outer_w.reshape(factors, factors, width)
    weight = lax.dynamic_slice_in_dim(weight, b * half, half, axis=1)
    weight = jnp.transpose(weight, (2, 1, 0)).reshape(width, half * factors)

    outers = shares // 4
    lanes = -(-(mine * (width // branches)) // 128) * 128
    stack = -(-(mine + heads_z) // 8) * 8
    f32 = jnp.float32
    dma = pltpu.SemaphoreType.DMA
    vmem = pl.BlockSpec(memory_space=pltpu.VMEM)
    args = (
        msa, mask, pair, place, factor_w, jnp.transpose(row_bias_w), weight,
        row_proj, row_out, start_proj, jnp.transpose(start_bias_w), start_out,
        end_proj, jnp.transpose(end_bias_w), end_out,
    )
    msa_o, pair_o = pl.pallas_call(
        functools.partial(block_kernel, local, branches, shares, heads, heads_z),
        out_shape=(
            jax.ShapeDtypeStruct((part, padded, features), f32),
            jax.ShapeDtypeStruct((everyone, padded, lanes), f32),
        ),
        in_specs=[vmem] * len(args),
        out_specs=(vmem, vmem),
        scratch_shapes=[
            pltpu.VMEM((local, factors, sequences), f32),
            pltpu.VMEM((half, padded, sequences), f32),
            pltpu.VMEM((padded, heads, spread), f32),
            pltpu.VMEM((local, spread, width), f32),
            pltpu.VMEM((shares, padded, features), f32),
            pltpu.VMEM((shares, half, padded, sequences), f32),
            pltpu.VMEM((shares, padded, heads, spread), f32),
            pltpu.VMEM((per_seq, shares, local, features), f32),
            pltpu.VMEM((per_seq, spread, features), f32),
            pltpu.VMEM((mine, spread, width), f32),
            pltpu.VMEM((mine, spread, width), f32),
            pltpu.VMEM((mine, spread, width), f32),
            pltpu.VMEM((mine, heads_z, spread), f32),
            pltpu.VMEM((spread, heads_z, spread), f32),
            pltpu.VMEM((everyone, mine, stack, width), f32),
            pltpu.VMEM((spread, stack, width), f32),
            pltpu.VMEM((heads_z, spread, spread), f32),
            pltpu.VMEM((branches, spread, lanes), f32),
            dma((3,)),
            dma((2, outers)),
            dma((2, outers)),
            dma((2, outers)),
            dma((2, outers)),
            dma((2, 2, outers)),
            dma((2, 2, outers)),
            dma((shares,)),
            dma((shares,)),
            dma((shares,)),
            dma((shares,)),
            dma,
            dma,
            dma((everyone,)),
            dma((everyone,)),
            dma((everyone,)),
            dma((everyone,)),
            dma((everyone,)),
            dma((everyone,)),
        ],
        compiler_params=pltpu.CompilerParams(
            collective_id=0, has_side_effects=True, vmem_limit_bytes=56 * 1024 * 1024
        ),
    )(*args)
    piece = width // branches
    pair_o = pair_o[:, :local, : mine * piece].reshape(everyone, local, mine, piece)
    pair_o = jnp.transpose(pair_o, (1, 0, 2, 3)).reshape(local, residues, piece)
    return msa_o[:, :local], pair_o


def per_device(
    msa,
    pair,
    msa_mask,
    residue_mask,
    row_proj,
    row_out,
    row_bias_w,
    first_w,
    other_w,
    outer_w,
    start_proj,
    start_bias_w,
    start_out,
    end_proj,
    end_bias_w,
    end_out,
):
    b = lax.axis_index("branch")
    branches = lax.axis_size("branch")
    shares = lax.axis_size("res")
    everyone = branches * shares
    sequences, local, features = msa.shape
    residues, width = pair.shape[1:]
    factors = first_w.shape[1]
    half = factors // branches
    mine = local // branches
    per_seq = sequences // everyone
    room = -(-(local + 1) // 8) * 8
    if shares * room == width and shares % 4 == 0 and width == 128:
        return fused(
            msa, pair, msa_mask, row_proj, row_out, row_bias_w, first_w, other_w, outer_w,
            start_proj, start_bias_w, start_out, end_proj, end_bias_w, end_out, room,
        )
    padded = -(-local // 8) * 8

    depth = jnp.sum(msa_mask, axis=0).astype(jnp.float32)
    bias_rows = project(layer_normalize(pair), row_bias_w, "ijc,ch->ihj")
    bias_pack = jnp.concatenate(
        [bias_rows, jnp.broadcast_to(depth[:, None, None], (local, 1, residues))], axis=1
    )

    normed = layer_normalize(msa)
    my_other = lax.dynamic_slice_in_dim(other_w, b * half, half, axis=1)
    mask = jnp.transpose(msa_mask).astype(jnp.float32)
    left = project(normed, first_w, "sia,ac->ics") * mask[:, None, :]
    right = project(normed, my_other, "sja,ae->ejs") * mask[None]
    right = jnp.pad(right, ((0, 0), (0, padded - local), (0, 0)))
    right_all = gather(right, "res", shares)

    bias_all = gather(bias_pack, "res", shares).reshape(residues, -1, residues)
    row_bias = jnp.transpose(bias_all[:, :-1], (1, 0, 2))
    depth_all = bias_all[:, -1, 0]

    my_msa = lax.dynamic_slice_in_dim(msa, b * (sequences // branches), sequences // branches, axis=0)
    seq_msa = lax.all_to_all(my_msa, "res", split_axis=0, concat_axis=1, tiled=True)

    weight = outer_w.reshape(factors, factors, width)
    weight = lax.dynamic_slice_in_dim(weight, b * half, half, axis=1)
    weight = jnp.transpose(weight, (2, 1, 0)).reshape(width, half * factors)
    partial = outer_product(left, right_all, weight)
    partial = partial.reshape(branches, mine, shares, padded, width)[:, :, :, :local]
    partial = partial.reshape(branches, mine, residues, width)
    update = jnp.sum(lax.all_to_all(partial, "branch", 0, 0), axis=0)
    my_depth = lax.dynamic_slice_in_dim(depth, b * mine, mine)
    overlap = jnp.minimum(my_depth[:, None], depth_all[None])
    my_pair = lax.dynamic_slice_in_dim(pair, b * mine, mine)
    pair_one = my_pair + update / jnp.maximum(overlap, 1.0)[:, :, None]

    start_rows = project(layer_normalize(pair_one), start_bias_w, "ijc,ch->ihj")
    start_all = gather(start_rows, EVERYONE, everyone)
    heads_z = start_bias_w.shape[1]
    start_score = jnp.transpose(start_all.reshape(residues, heads_z, residues), (1, 0, 2))
    live = jnp.broadcast_to((depth_all > 0.5).astype(jnp.float32), (mine, 1, residues))
    next_w = jnp.pad(jnp.transpose(end_bias_w), ((0, -heads_z % 8), (0, 0)))
    pair_two, end_rows = attention(
        pair_one, start_score, live, start_proj, start_out, heads_z, next_w
    )
    end_all = gather(end_rows[:, :heads_z], EVERYONE, everyone)
    end_score = jnp.transpose(end_all.reshape(residues, heads_z, residues), (1, 2, 0))

    columns = lax.all_to_all(
        pair_two.reshape(mine, everyone, mine, width), EVERYONE, 1, 0
    )
    columns = jnp.transpose(columns.reshape(residues, mine, width), (1, 0, 2))

    start_of_seq = (b * shares + lax.axis_index("res")) * per_seq
    present = (
        start_of_seq + jnp.arange(per_seq)[:, None, None] < depth_all[None, None, :]
    ).astype(jnp.float32)
    (seq_result,) = attention(
        seq_msa, row_bias, present, row_proj, row_out, row_bias_w.shape[1]
    )
    msa_result = lax.all_to_all(seq_result, "res", split_axis=1, concat_axis=0, tiled=True)

    (end_result,) = attention(columns, end_score, live, end_proj, end_out, heads_z)
    tiles = end_result.reshape(mine, shares, local, branches, width // branches)
    tiles = jnp.transpose(tiles, (1, 3, 2, 0, 4)).reshape(
        everyone, local, mine, width // branches
    )
    pair_result = lax.all_to_all(tiles, EVERYONE, 0, 0)
    pair_result = jnp.transpose(pair_result, (1, 0, 2, 3)).reshape(
        local, residues, width // branches
    )
    return msa_result, pair_result


def solution(mesh):
    in_specs = (
        P(None, "res", None),
        P("res", None, None),
        P(None, "res"),
        P("res"),
    ) + (P(),) * 12
    out_specs = (P("branch", "res", None), P("res", None, "branch"))
    return jax.shard_map(
        per_device, mesh=mesh, in_specs=in_specs, out_specs=out_specs, check_vma=False
    )
```

```python
import functools
import math

import jax
import jax.numpy as jnp
from jax import lax
from jax.experimental import pallas as pl
from jax.experimental.pallas import tpu as pltpu
from jax.sharding import PartitionSpec as P

epsilon = 1e-05
masked_score = -1000000000.0
EVERYONE = ("res", "branch")

NN = (((1,), (0,)), ((), ()))
NT = (((1,), (1,)), ((), ()))


def layer_normalize(values):
    centred = values - jnp.mean(values, axis=-1, keepdims=True)
    variance = jnp.mean(centred * centred, axis=-1, keepdims=True)
    return centred * lax.rsqrt(variance + epsilon)


def split(values):
    high = values.astype(jnp.bfloat16)
    return high, (values - high.astype(jnp.float32)).astype(jnp.bfloat16)


def dot3(a, b, dims=NN):
    (ah, al), (bh, bl) = a, b

    def one(x, y):
        return lax.dot_general(x, y, dims, preferred_element_type=jnp.float32)

    return one(ah, bh) + (one(ah, bl) + one(al, bh))


def attention_kernel(heads, x_ref, bias_ref, live_ref, proj_ref, out_w_ref, *rest):
    next_w_ref, o_ref, next_ref = rest if len(rest) == 3 else (None, rest[0], None)
    x = x_ref[0]
    channels = x.shape[1]
    width = channels // heads
    normed = split(layer_normalize(x))
    q, k, v, g = (dot3(normed, split(proj_ref[p])) for p in range(4))
    q = q * (1.0 / math.sqrt(width))
    keys = split(k)
    owner = lax.broadcasted_iota(jnp.int32, (1, channels), 1) // width
    live = live_ref[0] > 0.5
    mixture = None
    for h in range(heads):
        mine = owner == h
        scores = dot3(split(jnp.where(mine, q, 0.0)), keys, NT) + bias_ref[h]
        scores = jnp.where(live, scores, masked_score)
        weights = jnp.exp(scores - jnp.max(scores, axis=-1, keepdims=True))
        weights = weights / jnp.sum(weights, axis=-1, keepdims=True)
        term = dot3(split(weights), split(jnp.where(mine, v, 0.0)))
        mixture = term if mixture is None else mixture + term
    gated = jax.nn.sigmoid(g) * mixture
    result = x + dot3(split(gated), split(out_w_ref[...]))
    o_ref[0] = result
    if next_ref is not None:
        next_ref[0] = dot3(split(next_w_ref[...]), split(layer_normalize(result)), NT)


def attention(x, bias, live, proj, out_w, heads, next_w=None):
    lines, residues, channels = x.shape

    def whole(a):
        return pl.BlockSpec(a.shape, lambda i: (0,) * a.ndim)

    line = pl.BlockSpec((1, residues, channels), lambda i: (i, 0, 0))
    args = [x, bias, live, proj, out_w]
    in_specs = [
        line,
        whole(bias),
        pl.BlockSpec((1, 1, residues), lambda i: (i, 0, 0)),
        whole(proj),
        whole(out_w),
    ]
    out_shape = [jax.ShapeDtypeStruct(x.shape, jnp.float32)]
    out_specs = [line]
    if next_w is not None:
        args.append(next_w)
        in_specs.append(whole(next_w))
        out_shape.append(
            jax.ShapeDtypeStruct((lines, next_w.shape[0], residues), jnp.float32)
        )
        out_specs.append(
            pl.BlockSpec((1, next_w.shape[0], residues), lambda i: (i, 0, 0))
        )
    return pl.pallas_call(
        functools.partial(attention_kernel, heads),
        grid=(lines,),
        in_specs=in_specs,
        out_specs=out_specs,
        out_shape=out_shape,
    )(*args)


def outer_kernel(left_ref, right_ref, weight_ref, o_ref):
    rows, factors, sequences = left_ref.shape
    shares, half, padded, _ = right_ref.shape
    columns = shares * padded
    left = split(left_ref[...].reshape(rows * factors, sequences))
    weight = split(weight_ref[...])
    products = []
    for e in range(half):
        right = split(right_ref[:, e].reshape(columns, sequences))
        products.append(dot3(left, right, NT))
    for i in range(rows):
        block = jnp.concatenate(
            [one[i * factors : (i + 1) * factors] for one in products], axis=0
        )
        o_ref[i] = jnp.transpose(dot3(weight, split(block)))


def outer_product(left, right, weight):
    rows = left.shape[0]
    columns = right.shape[0] * right.shape[2]
    return pl.pallas_call(
        outer_kernel,
        out_shape=jax.ShapeDtypeStruct((rows, columns, weight.shape[0]), jnp.float32),
    )(left, right, weight)


def project(a, b, form):
    return jnp.einsum(form, a, b, precision=lax.Precision.HIGH)


def gather(block, axes, count):
    copies = jnp.broadcast_to(block[None], (count,) + block.shape)
    return lax.all_to_all(copies, axes, 0, 0)


MESH = pl.DeviceIdType.MESH


def rows_attention(x, bias_of, mask_of, proj, out_w, heads):
    lines, channels = x.shape
    width = channels // heads
    tile = 128
    per_tile = tile // width
    normed = split(layer_normalize(x))
    q, k, v, g = (dot3(normed, split(proj[p])) for p in range(4))
    q = q * (1.0 / math.sqrt(width))
    owner = lax.broadcasted_iota(jnp.int32, (1, tile), 1) // width
    bf16 = jnp.bfloat16
    mixtures = []
    for first in range(0, channels, tile):

        def halves(values):
            values = values[:, first : first + tile]
            high = values.astype(bf16).astype(jnp.float32)
            return high, values - high

        (q_hi, q_lo), (k_hi, k_lo), (v_hi, v_lo) = halves(q), halves(k), halves(v)
        q_turn = pltpu.roll(q_hi, width, 1)
        k_turn = pltpu.roll(k_lo, width, 1)
        keys = [
            jnp.concatenate(
                [k_hi, jnp.where(owner % 2 == parity, k_hi, k_turn)], axis=1
            ).astype(bf16)
            for parity in range(2)
        ]
        total = None
        for n in range(per_tile):
            mine, after = owner == n, owner == (n + 1) % per_tile
            query = jnp.concatenate(
                [
                    jnp.where(mine, q_hi, 0.0),
                    jnp.where(mine, q_lo, jnp.where(after, q_turn, 0.0)),
                ],
                axis=1,
            ).astype(bf16)
            scores = lax.dot_general(
                query, keys[n % 2], NT, preferred_element_type=jnp.float32
            )
            scores = mask_of(scores + bias_of(first // width + n))
            weights = jnp.exp(scores - jnp.max(scores, axis=-1, keepdims=True))
            weights = weights / jnp.sum(weights, axis=-1, keepdims=True)
            w_hi, w_lo = split(weights)
            m_hi = jnp.where(mine, v_hi, 0.0).astype(bf16)
            m_lo = jnp.where(mine, v_lo, 0.0).astype(bf16)
            values = jnp.concatenate(
                [
                    jnp.concatenate([m_hi, m_lo], axis=1),
                    jnp.concatenate([m_hi, jnp.zeros_like(m_lo)], axis=1),
                ],
                axis=0,
            )
            term = lax.dot_general(
                jnp.concatenate([w_hi, w_lo], axis=1),
                values,
                NN,
                preferred_element_type=jnp.float32,
            )
            total = term if total is None else total + term
        mixtures.append(total[:, :tile] + total[:, tile:])
    mixture = mixtures[0] if len(mixtures) == 1 else jnp.concatenate(mixtures, axis=1)
    return x + dot3(split(jax.nn.sigmoid(g) * mixture), split(out_w[...]))


def block_kernel(
    local,
    branches,
    shares,
    heads,
    heads_z,
    msa_ref,
    mask_ref,
    wide_ref,
    place_ref,
    factor_w,
    bias_w,
    outer_ref,
    row_proj,
    row_out,
    start_proj,
    start_w,
    start_out,
    end_proj,
    end_w,
    end_out,
    msa_o,
    pair_o,
    left_ref,
    right_ref,
    bias_ref,
    pair_ref,
    seq_pad,
    right_all,
    bias_all,
    seq_in,
    seq_res,
    part_out,
    part_in,
    pair_one,
    start_send,
    start_all,
    tile_send,
    tile_all,
    column_in,
    pair_send,
    own_sem,
    ag_send,
    ag_recv,
    x_send,
    x_recv,
    c_send,
    c_recv,
    in_send,
    in_recv,
    out_send,
    out_recv,
    y_send,
    y_recv,
    s_send,
    s_recv,
    t_send,
    t_recv,
    p_send,
    p_recv,
):
    b = lax.axis_index("branch")
    r = lax.axis_index("res")
    everyone = branches * shares
    me = r * branches + b
    mine = local // branches
    per_seq = seq_in.shape[0]
    padded = right_ref.shape[1]
    residues = shares * padded
    factors = left_ref.shape[1]
    half = right_ref.shape[0]
    outers = shares // 4
    outer, inner = r // 4, r % 4
    twin_x = outer * 4 + (inner + 2) % 4
    twin_c = outer * 4 + (inner // 2) * 2 + (inner + 1) % 2
    my_rows = r * padded + b * mine

    def remote(src, dst, send, recv, branch, res):
        return pltpu.make_async_remote_copy(
            src_ref=src,
            dst_ref=dst,
            send_sem=send,
            recv_sem=recv,
            device_id={"branch": branch, "res": res},
            device_id_type=MESH,
        )

    def each(low, high, body):
        def step(k, carry):
            body(k)
            return carry

        lax.fori_loop(low, high, step, 0)

    start_all[...] = jnp.zeros_like(start_all)
    tile_all[...] = jnp.zeros_like(tile_all)
    right_ref[...] = jnp.zeros_like(right_ref)
    bias_ref[...] = jnp.zeros_like(bias_ref)
    seq_pad[...] = jnp.zeros_like(seq_pad)
    pair_ref[...] = jnp.zeros_like(pair_ref)

    barrier = pltpu.get_barrier_semaphore()

    def greet(k):
        other = (me + k) % everyone
        pl.semaphore_signal(
            barrier,
            inc=1,
            device_id={"branch": other % branches, "res": other // branches},
            device_id_type=MESH,
        )

    each(1, everyone, greet)

    factor = split(factor_w[...])
    for j in range(local):
        line = split(layer_normalize(msa_ref[:, j, :]))
        both = dot3(factor, line, NT) * mask_ref[j : j + 1]
        left_ref[j] = both[:factors]
        right_ref[:, j, :] = both[factors:]
    for i in range(local):
        for share in range(shares):
            pair_ref[i, share * padded : share * padded + local, :] = wide_ref[
                i, share * local : (share + 1) * local, :
            ]
    weight = split(bias_w[...])
    for i in range(local):
        bias_ref[i] = dot3(weight, split(layer_normalize(pair_ref[i])), NT)
    right_ref[0, local : local + 1, :] = place_ref[...]
    pl.semaphore_wait(barrier, everyone - 1)

    pairs = ((right_ref, right_all, 0), (bias_ref, bias_all, 1))

    def stage_one(k, which):
        source, target, n = which
        peer = ((outer + k) % outers) * 4 + inner
        return remote(source, target.at[r], ag_send.at[n, k], ag_recv.at[n, k], b, peer)

    def stage_two(k, which):
        _, target, n = which
        at = ((outer + outers - k) % outers) * 4 + inner
        return remote(
            target.at[at], target.at[at], x_send.at[n, k], x_recv.at[n, k], b, twin_x
        )

    def stage_three(k, side, which):
        _, target, n = which
        at = ((outer + outers - k) % outers) * 4 + (inner + 2 * side) % 4
        return remote(
            target.at[at],
            target.at[at],
            c_send.at[n, side, k],
            c_recv.at[n, side, k],
            b,
            twin_c,
        )

    def seq_copy(k):
        peer = (r + k) % shares
        return remote(
            msa_ref.at[pl.ds((b * shares + peer) * per_seq, per_seq)],
            seq_in.at[:, r],
            in_send.at[k],
            in_recv.at[k],
            b,
            peer,
        )

    own = [
        pltpu.make_async_copy(right_ref, right_all.at[r], own_sem.at[0]),
        pltpu.make_async_copy(bias_ref, bias_all.at[r], own_sem.at[1]),
        pltpu.make_async_copy(
            msa_ref.at[pl.ds((b * shares + r) * per_seq, per_seq)], seq_in.at[:, r], own_sem.at[2]
        ),
    ]
    for copy in own:
        copy.start()
    def forward(which):
        def one(k):
            stage_one(k, which).wait()
            stage_two(k, which).start()
            stage_three(k, 0, which).start()

        def across(k):
            stage_two(k, which).wait()
            stage_three(k, 1, which).start()

        def finish(k):
            stage_three(k, 0, which).wait()
            stage_three(k, 1, which).wait()

        each(1, outers, one)
        each(0, outers, across)
        each(0, outers, finish)

    each(1, outers, lambda k: stage_one(k, pairs[0]).start())
    for copy in own:
        copy.wait()
    stage_two(0, pairs[0]).start()
    stage_three(0, 0, pairs[0]).start()
    forward(pairs[0])
    each(1, outers, lambda k: stage_one(k, pairs[1]).start())
    stage_two(0, pairs[1]).start()
    stage_three(0, 0, pairs[1]).start()
    each(1, shares, lambda k: seq_copy(k).start())

    other_b = (b + 1) % branches
    left = jnp.concatenate(
        [left_ref[pl.ds(other_b * mine, mine)], left_ref[pl.ds(b * mine, mine)]], axis=0
    ).reshape(local * factors, left_ref.shape[2])
    left = split(left)
    weight = split(outer_ref[...])
    products = []
    for e in range(half):
        right = split(right_all[:, e].reshape(residues, right_all.shape[3]))
        products.append(dot3(left, right, NT))

    def outer_row(i):
        block = jnp.concatenate(
            [one[i * factors : (i + 1) * factors] for one in products], axis=0
        )
        return jnp.transpose(dot3(weight, split(block)))

    for i in range(mine):
        part_out[i] = outer_row(i)
    swap = remote(part_out, part_in, y_send, y_recv, other_b, r)
    swap.start()
    for i in range(mine):
        pair_one[i] = outer_row(mine + i)

    depth = jnp.sum(right_all[:, 0, local, :], axis=0, keepdims=True)
    depth_rows = jnp.transpose(jnp.broadcast_to(depth, (residues, residues)))
    lane = lax.broadcasted_iota(jnp.int32, (1, residues), 1)
    dead = jnp.where(lane % padded < local, masked_score, 3.0 * masked_score)
    present = depth > 0.5

    def pair_mask(scores):
        return jnp.where(present, scores, dead)

    first_seq = ((b * shares + r) * per_seq).astype(jnp.float32)

    def row_sequence(s):
        live = depth > first_seq + s.astype(jnp.float32)
        seq_pad[:, :local, :] = seq_in[s]
        x = seq_pad[...].reshape(residues, seq_in.shape[3])
        result = rows_attention(
            x,
            lambda h: bias_all[:, :, h, :].reshape(residues, residues),
            lambda scores: jnp.where(live, scores, dead),
            row_proj,
            row_out,
            heads,
        )
        seq_res[s] = result.reshape(shares, padded, seq_in.shape[3])[:, :local, :]

    column_in[0] = depth_rows
    swap.wait()
    for i in range(mine):
        update = pair_one[i] + part_in[i]
        overlap = jnp.maximum(jnp.minimum(depth_rows, column_in[0, pl.ds(my_rows + i, 1), :]), 1.0)
        pair_one[i] = pair_ref[b * mine + i] + update / overlap
        start_send[i] = dot3(
            split(start_w[...]), split(layer_normalize(pair_one[i])), NT
        )

    def start_copy(k):
        other = (me + k) % everyone
        return remote(
            start_send,
            start_all.at[pl.ds(my_rows, mine)],
            s_send.at[k],
            s_recv.at[k],
            other % branches,
            other // branches,
        )

    each(1, everyone, lambda k: start_copy(k).start())
    own = pltpu.make_async_copy(
        start_send, start_all.at[pl.ds(my_rows, mine)], own_sem.at[0]
    )
    own.start()

    forward(pairs[1])
    each(1, shares, lambda k: seq_copy(k).wait())
    early = per_seq // 2
    each(0, early, row_sequence)

    def row_copy(k, late):
        peer = (r + k) % shares
        at, count = (early, per_seq - early) if late else (0, early)
        return remote(
            seq_res.at[pl.ds(at, count), peer],
            msa_o.at[pl.ds(r * per_seq + at, count)],
            out_send.at[late, k],
            out_recv.at[late, k],
            b,
            peer,
        )

    own.wait()
    each(1, everyone, lambda k: start_copy(k).wait())
    each(1, shares, lambda k: row_copy(k, 0).start())

    for i in range(mine):
        two = rows_attention(
            pair_one[i],
            lambda h: start_all[:, h, :],
            pair_mask,
            start_proj,
            start_out,
            heads_z,
        )
        rows = dot3(split(end_w[...]), split(layer_normalize(two)), NT)
        for d in range(everyone):
            at = (d // branches) * padded + (d % branches) * mine
            tile_send[d, i, :mine] = two[at : at + mine]
            tile_send[d, i, mine : mine + heads_z] = rows

    def tile_copy(k):
        other = (me + k) % everyone
        return remote(
            tile_send.at[other],
            tile_all.at[pl.ds(my_rows, mine)],
            t_send.at[k],
            t_recv.at[k],
            other % branches,
            other // branches,
        )

    each(1, everyone, lambda k: tile_copy(k).start())
    own = pltpu.make_async_copy(
        tile_send.at[me], tile_all.at[pl.ds(my_rows, mine)], own_sem.at[0]
    )
    own.start()
    each(early, per_seq, row_sequence)

    own.wait()
    each(1, everyone, lambda k: tile_copy(k).wait())
    each(1, shares, lambda k: row_copy(k, 1).start())
    own_row = pltpu.make_async_copy(
        seq_res.at[:, r], msa_o.at[pl.ds(r * per_seq, per_seq)], own_sem.at[1]
    )
    own_row.start()

    width = pair_ref.shape[2]
    share = width // branches
    for h in range(heads_z):
        column_in[h] = jnp.transpose(tile_all[:, mine + h, :])
    results = []
    for i in range(mine):
        results.append(
            rows_attention(
                tile_all[:, i, :],
                lambda h: column_in[h],
                pair_mask,
                end_proj,
                end_out,
                heads_z,
            )
        )
    for c in range(branches):
        pair_send[c] = jnp.concatenate(
            [one[:, c * share : (c + 1) * share] for one in results]
            + [jnp.zeros((residues, pair_send.shape[2] - mine * share), jnp.float32)],
            axis=1,
        )

    def pair_copy(k):
        other = (me + k) % everyone
        at = pl.multiple_of((other // branches) * padded, padded)
        return remote(
            pair_send.at[other % branches, pl.ds(at, padded), :],
            pair_o.at[me],
            p_send.at[k],
            p_recv.at[k],
            other % branches,
            other // branches,
        )

    each(1, everyone, lambda k: pair_copy(k).start())
    own = pltpu.make_async_copy(
        pair_send.at[b, pl.ds(pl.multiple_of(r * padded, padded), padded), :],
        pair_o.at[me],
        own_sem.at[0],
    )
    own.start()
    own.wait()
    own_row.wait()
    each(1, shares, lambda k: row_copy(k, 0).wait())
    each(1, shares, lambda k: row_copy(k, 1).wait())
    each(1, everyone, lambda k: pair_copy(k).wait())


def fused(
    msa, pair, msa_mask, row_proj, row_out, row_bias_w, first_w, other_w, outer_w,
    start_proj, start_bias_w, start_out, end_proj, end_bias_w, end_out, padded,
):
    b = lax.axis_index("branch")
    r = lax.axis_index("res")
    branches = lax.axis_size("branch")
    shares = lax.axis_size("res")
    everyone = branches * shares
    sequences, local, features = msa.shape
    residues, width = pair.shape[1:]
    factors = first_w.shape[1]
    half = factors // branches
    mine = local // branches
    per_seq = sequences // everyone
    spread = shares * padded
    heads, heads_z = row_bias_w.shape[1], start_bias_w.shape[1]

    mask = jnp.transpose(msa_mask).astype(jnp.float32)
    depth = jnp.sum(mask, axis=1)
    place = lax.dynamic_update_slice(
        jnp.zeros((1, spread), jnp.float32), depth[None], (0, r * padded)
    )
    my_other = lax.dynamic_slice_in_dim(other_w, b * half, half, axis=1)
    factor_w = jnp.transpose(jnp.concatenate([first_w, my_other], axis=1))
    part = sequences // branches
    weight = outer_w.reshape(factors, factors, width)
    weight = lax.dynamic_slice_in_dim(weight, b * half, half, axis=1)
    weight = jnp.transpose(weight, (2, 1, 0)).reshape(width, half * factors)

    outers = shares // 4
    lanes = -(-(mine * (width // branches)) // 128) * 128
    stack = -(-(mine + heads_z) // 8) * 8
    f32 = jnp.float32
    dma = pltpu.SemaphoreType.DMA
    vmem = pl.BlockSpec(memory_space=pltpu.VMEM)
    args = (
        msa, mask, pair, place, factor_w, jnp.transpose(row_bias_w), weight,
        row_proj, row_out, start_proj, jnp.transpose(start_bias_w), start_out,
        end_proj, jnp.transpose(end_bias_w), end_out,
    )
    msa_o, pair_o = pl.pallas_call(
        functools.partial(block_kernel, local, branches, shares, heads, heads_z),
        out_shape=(
            jax.ShapeDtypeStruct((part, local, features), f32),
            jax.ShapeDtypeStruct((everyone, padded, lanes), f32),
        ),
        in_specs=[vmem] * len(args),
        out_specs=(vmem, vmem),
        scratch_shapes=[
            pltpu.VMEM((local, factors, sequences), f32),
            pltpu.VMEM((half, padded, sequences), f32),
            pltpu.VMEM((padded, heads, spread), f32),
            pltpu.VMEM((local, spread, width), f32),
            pltpu.VMEM((shares, padded, features), f32),
            pltpu.VMEM((shares, half, padded, sequences), f32),
            pltpu.VMEM((shares, padded, heads, spread), f32),
            pltpu.VMEM((per_seq, shares, local, features), f32),
            pltpu.VMEM((per_seq, shares, local, features), f32),
            pltpu.VMEM((mine, spread, width), f32),
            pltpu.VMEM((mine, spread, width), f32),
            pltpu.VMEM((mine, spread, width), f32),
            pltpu.VMEM((mine, heads_z, spread), f32),
            pltpu.VMEM((spread, heads_z, spread), f32),
            pltpu.VMEM((everyone, mine, stack, width), f32),
            pltpu.VMEM((spread, stack, width), f32),
            pltpu.VMEM((heads_z, spread, spread), f32),
            pltpu.VMEM((branches, spread, lanes), f32),
            dma((3,)),
            dma((2, outers)),
            dma((2, outers)),
            dma((2, outers)),
            dma((2, outers)),
            dma((2, 2, outers)),
            dma((2, 2, outers)),
            dma((shares,)),
            dma((shares,)),
            dma((2, shares)),
            dma((2, shares)),
            dma,
            dma,
            dma((everyone,)),
            dma((everyone,)),
            dma((everyone,)),
            dma((everyone,)),
            dma((everyone,)),
            dma((everyone,)),
        ],
        compiler_params=pltpu.CompilerParams(
            collective_id=0, has_side_effects=True, vmem_limit_bytes=56 * 1024 * 1024
        ),
    )(*args)
    piece = width // branches
    pair_o = pair_o[:, :local, : mine * piece].reshape(everyone, local, mine, piece)
    pair_o = jnp.transpose(pair_o, (1, 0, 2, 3)).reshape(local, residues, piece)
    return msa_o, pair_o


def per_device(
    msa,
    pair,
    msa_mask,
    residue_mask,
    row_proj,
    row_out,
    row_bias_w,
    first_w,
    other_w,
    outer_w,
    start_proj,
    start_bias_w,
    start_out,
    end_proj,
    end_bias_w,
    end_out,
):
    b = lax.axis_index("branch")
    branches = lax.axis_size("branch")
    shares = lax.axis_size("res")
    everyone = branches * shares
    sequences, local, features = msa.shape
    residues, width = pair.shape[1:]
    factors = first_w.shape[1]
    half = factors // branches
    mine = local // branches
    per_seq = sequences // everyone
    room = -(-(local + 1) // 8) * 8
    if shares * room == width == sequences == 128 and shares % 4 == 0:
        return fused(
            msa, pair, msa_mask, row_proj, row_out, row_bias_w, first_w, other_w, outer_w,
            start_proj, start_bias_w, start_out, end_proj, end_bias_w, end_out, room,
        )
    padded = -(-local // 8) * 8

    depth = jnp.sum(msa_mask, axis=0).astype(jnp.float32)
    bias_rows = project(layer_normalize(pair), row_bias_w, "ijc,ch->ihj")
    bias_pack = jnp.concatenate(
        [bias_rows, jnp.broadcast_to(depth[:, None, None], (local, 1, residues))], axis=1
    )

    normed = layer_normalize(msa)
    my_other = lax.dynamic_slice_in_dim(other_w, b * half, half, axis=1)
    mask = jnp.transpose(msa_mask).astype(jnp.float32)
    left = project(normed, first_w, "sia,ac->ics") * mask[:, None, :]
    right = project(normed, my_other, "sja,ae->ejs") * mask[None]
    right = jnp.pad(right, ((0, 0), (0, padded - local), (0, 0)))
    right_all = gather(right, "res", shares)

    bias_all = gather(bias_pack, "res", shares).reshape(residues, -1, residues)
    row_bias = jnp.transpose(bias_all[:, :-1], (1, 0, 2))
    depth_all = bias_all[:, -1, 0]

    my_msa = lax.dynamic_slice_in_dim(msa, b * (sequences // branches), sequences // branches, axis=0)
    seq_msa = lax.all_to_all(my_msa, "res", split_axis=0, concat_axis=1, tiled=True)

    weight = outer_w.reshape(factors, factors, width)
    weight = lax.dynamic_slice_in_dim(weight, b * half, half, axis=1)
    weight = jnp.transpose(weight, (2, 1, 0)).reshape(width, half * factors)
    partial = outer_product(left, right_all, weight)
    partial = partial.reshape(branches, mine, shares, padded, width)[:, :, :, :local]
    partial = partial.reshape(branches, mine, residues, width)
    update = jnp.sum(lax.all_to_all(partial, "branch", 0, 0), axis=0)
    my_depth = lax.dynamic_slice_in_dim(depth, b * mine, mine)
    overlap = jnp.minimum(my_depth[:, None], depth_all[None])
    my_pair = lax.dynamic_slice_in_dim(pair, b * mine, mine)
    pair_one = my_pair + update / jnp.maximum(overlap, 1.0)[:, :, None]

    start_rows = project(layer_normalize(pair_one), start_bias_w, "ijc,ch->ihj")
    start_all = gather(start_rows, EVERYONE, everyone)
    heads_z = start_bias_w.shape[1]
    start_score = jnp.transpose(start_all.reshape(residues, heads_z, residues), (1, 0, 2))
    live = jnp.broadcast_to((depth_all > 0.5).astype(jnp.float32), (mine, 1, residues))
    next_w = jnp.pad(jnp.transpose(end_bias_w), ((0, -heads_z % 8), (0, 0)))
    pair_two, end_rows = attention(
        pair_one, start_score, live, start_proj, start_out, heads_z, next_w
    )
    end_all = gather(end_rows[:, :heads_z], EVERYONE, everyone)
    end_score = jnp.transpose(end_all.reshape(residues, heads_z, residues), (1, 2, 0))

    columns = lax.all_to_all(
        pair_two.reshape(mine, everyone, mine, width), EVERYONE, 1, 0
    )
    columns = jnp.transpose(columns.reshape(residues, mine, width), (1, 0, 2))

    start_of_seq = (b * shares + lax.axis_index("res")) * per_seq
    present = (
        start_of_seq + jnp.arange(per_seq)[:, None, None] < depth_all[None, None, :]
    ).astype(jnp.float32)
    (seq_result,) = attention(
        seq_msa, row_bias, present, row_proj, row_out, row_bias_w.shape[1]
    )
    msa_result = lax.all_to_all(seq_result, "res", split_axis=1, concat_axis=0, tiled=True)

    (end_result,) = attention(columns, end_score, live, end_proj, end_out, heads_z)
    tiles = end_result.reshape(mine, shares, local, branches, width // branches)
    tiles = jnp.transpose(tiles, (1, 3, 2, 0, 4)).reshape(
        everyone, local, mine, width // branches
    )
    pair_result = lax.all_to_all(tiles, EVERYONE, 0, 0)
    pair_result = jnp.transpose(pair_result, (1, 0, 2, 3)).reshape(
        local, residues, width // branches
    )
    return msa_result, pair_result


def solution(mesh):
    in_specs = (
        P(None, "res", None),
        P("res", None, None),
        P(None, "res"),
        P("res"),
    ) + (P(),) * 12
    out_specs = (P("branch", "res", None), P("res", None, "branch"))
    return jax.shard_map(
        per_device, mesh=mesh, in_specs=in_specs, out_specs=out_specs, check_vma=False
    )
```
